512 devices in a mesh: dp: 16 (over z, core), ctx: 32 (over x, y).
Axes of the slice: x: 4, y: 8, z: 8, core: 2. Of those that a mesh axis runs over, the one named last changes fastest.
Arguments:
- signal: bfloat16 [16, 1024, 4096], P('dp', None, 'ctx'), may hold values from -6 to 6
- gate: bfloat16 [16, 1024, 4096], P('dp', None, 'ctx'), may hold values from -6 to 6
- cotangent: bfloat16 [16, 1024, 4096], P('dp', None, 'ctx'), may hold values from -6 to 6
- w_in: bfloat16 [64, 33], replicated, may hold values from -1 to 1
- w_mid: bfloat16 [64, 64], replicated, may hold values from -0.75 to 0.75
- w_out: bfloat16 [1024, 64], replicated, may hold values from -0.75 to 0.75
- rates: float32 [1024], replicated, may hold values from 1 to 30
- skip: float32 [1024], replicated, may hold values from -4 to 4
- lengths: int32 [1024], replicated, may hold values from 32 to 4096
- owner: int32 [1024], replicated, may hold values from 0 to 31, as said below
Outputs:
- result: bfloat16 [16, 1024, 4096], P('dp', None, 'ctx')
- d_gate: bfloat16 [16, 1024, 4096], P('dp', None, 'ctx')
- d_signal: bfloat16 [16, 1024, 4096], P('dp', None, 'ctx')
- tap_grad: float32 [2048, 4096], P('ctx', 'dp')
The draws below stay inside these ranges and needn't reach their ends.
Inputs may be any that keep to these rules, and one draw needn't show every extreme that they name: `owner`: each index of ctx owns at most 64 channels, and in every draw some index owns exactly 64.
All inputs are finite; a program needn't handle non-finite values.
Results may differ from the reference program's by a relative error of at most 0.0036.
Values may be sent and summed in bfloat16 or wider, within the bound.
No kernel may reach another device: no remote copies, remote signals or barrier semaphores. Data moves between devices by JAX's collectives and lax.ppermute only.
A program may use at most 64 MiB of HBM per device.

```python
import math
import jax
import jax.numpy as jnp
from jax import lax

D = 1024
EMB = 33
HID = 64
L = 4096
BATCH = 16
C_DEV = 32
CAP = 64


def draw_lengths(key, part):
    first, second, third = jax.random.split(key, 3)
    levels = (L // 32).bit_length() - 1
    exponent = jax.random.randint(first, (D,), 0, levels)
    lowest = jnp.left_shift(jnp.int32(32), exponent)
    surplus = jax.random.randint(second, (D,), 0, lowest)
    result = lowest + surplus
    chosen = jax.random.permutation(third, D)
    result = result.at[chosen[0]].set(L).at[chosen[1]].set(32)
    return result.astype(jnp.int32)


def draw_owner(key, part):
    first, second, third = jax.random.split(key, 3)
    holders = D // C_DEV
    pair_count = holders // 2
    moved = jax.random.randint(first, (pair_count,), 0, C_DEV + 1).at[0].set(C_DEV)
    loads = jnp.stack([C_DEV + moved, C_DEV - moved], axis=1).reshape(holders)
    loads = loads[jax.random.permutation(second, holders)]
    bounds = jnp.cumsum(loads)
    places = jnp.arange(D, dtype=jnp.int32)
    holder_of = jnp.sum((places[:, None] >= bounds[None, :]).astype(jnp.int32), axis=1)
    order = jax.random.permutation(third, D)
    return jnp.zeros((D,), jnp.int32).at[order].set(holder_of.astype(jnp.int32))


def level_of(stream_key, shape, pieces, smallest, high):
    def one(axis_at, shards_of):
        heights = jax.random.uniform(jax.random.fold_in(jax.random.fold_in(stream_key, 6), axis_at), (shards_of,), jnp.float32, smallest / len(pieces), high / len(pieces))
        return jnp.repeat(jnp.exp(heights), shape[axis_at] // shards_of).reshape((-1,) + (1,) * (len(shape) - axis_at - 1))

    loudness = one(*pieces[0])
    for cut in pieces[1:]:
        loudness = loudness * one(*cut)
    return loudness


def scatter_about(own_key, shape, width, bound, cuts=(), kind=jnp.bfloat16):
    drawn = width * jax.random.normal(own_key, shape, jnp.float32)
    if cuts:
        drawn = drawn * level_of(own_key, shape, cuts, -0.22, 0.18)
    return jnp.clip(drawn, -bound, bound).astype(kind)


def setup_inputs(seed: int = 0) -> dict:
    splits = jax.random.split(jax.random.key(seed), 11)
    signal = scatter_about(splits[0], (BATCH, D, L), 1.0, 6.0, ((0, 16), (2, 32)))
    gate = scatter_about(splits[1], (BATCH, D, L), 1.0, 6.0, ((0, 16), (2, 32)))
    cotangent = scatter_about(splits[2], (BATCH, D, L), 1.0, 6.0, ((0, 16), (2, 32)))
    w_in = scatter_about(splits[3], (HID, EMB), EMB ** -0.5, 1.0)
    w_mid = scatter_about(splits[4], (HID, HID), HID ** -0.5, 0.75)
    w_out = scatter_about(splits[5], (D, HID), HID ** -0.5, 0.75)
    rates = jnp.clip(jnp.exp(jax.random.uniform(splits[6], (D,), jnp.float32, math.log(1.0), math.log(30.0))), 1.0, 30.0)
    skip = scatter_about(splits[7], (D,), 1.0, 4.0, (), jnp.float32)
    lengths = draw_lengths(jax.random.fold_in(splits[10], 71), 0)
    owner = draw_owner(jax.random.fold_in(splits[10], 71), 0)
    return dict(signal=signal, gate=gate, cotangent=cotangent, w_in=w_in, w_mid=w_mid, w_out=w_out, rates=rates, skip=skip, lengths=lengths, owner=owner)


def embed_points(points, seq_total, bands):
    freq_ids = jnp.arange(1, bands + 1, dtype=jnp.int32)
    phase = (freq_ids[:, None] * points[None, :] % seq_total).astype(jnp.float32) * (2.0 * math.pi / seq_total)
    ramp = points.astype(jnp.float32)[None, :] / seq_total
    return jnp.concatenate([ramp, jnp.cos(phase), jnp.sin(phase)], axis=0).astype(jnp.bfloat16)

def filter_rows(points, w_in, w_mid, w_out_rows, rate_rows, length_rows, seq_total):
    embedded = embed_points(points, seq_total, (w_in.shape[1] - 1) // 2)
    act_one = jnp.sin(jnp.dot(w_in, embedded, preferred_element_type=jnp.float32)).astype(jnp.bfloat16)
    act_two = jnp.sin(jnp.dot(w_mid, act_one, preferred_element_type=jnp.float32)).astype(jnp.bfloat16)
    network = jnp.dot(w_out_rows, act_two, preferred_element_type=jnp.float32)
    moments = points.astype(jnp.float32)
    decay = jnp.exp(-rate_rows[:, None] * moments[None, :] / seq_total)
    scaling = lax.rsqrt(length_rows.astype(jnp.float32))
    inside = points[None, :] < length_rows[:, None]
    return jnp.where(inside, network * decay * scaling[:, None], 0.0).astype(jnp.bfloat16)

def slot_layout(owner, holders, capacity):
    onehot = (owner[:, None] == jnp.arange(holders, dtype=jnp.int32)[None, :]).astype(jnp.int32)
    running = jnp.cumsum(onehot, axis=0)
    within = lax.optimization_barrier(jnp.sum(running * onehot, axis=1)) - 1
    slot_pos = (owner * capacity + within).astype(jnp.int32)
    slot_chan = jnp.zeros((holders * capacity,), jnp.int32).at[slot_pos].set(jnp.arange(owner.shape[0], dtype=jnp.int32))
    filled = jnp.zeros((holders * capacity,), jnp.float32).at[slot_pos].set(1.0)
    return (slot_pos, slot_chan, filled)

def reference(signal, gate, cotangent, w_in, w_mid, w_out, rates, skip, lengths, owner):
    sequences, channels, seq_len = signal.shape
    length_two = 2 * seq_len
    points = jnp.arange(seq_len, dtype=jnp.int32)
    taps = filter_rows(points, w_in, w_mid, w_out, rates, lengths, seq_len)
    tap_spec = jnp.fft.rfft(taps.astype(jnp.float32), n=length_two, axis=1)
    skip_col = skip[:, None]

    def one_context(summed, inputs):
        sig_rows, gate_rows, cot_rows = inputs
        sig_wide = sig_rows.astype(jnp.float32)
        gate_wide = gate_rows.astype(jnp.float32)
        cot_wide = cot_rows.astype(jnp.float32)
        sig_spec = jnp.fft.rfft(sig_wide, n=length_two, axis=1)
        conv = jnp.fft.irfft(sig_spec * tap_spec, n=length_two, axis=1)[:, :seq_len]
        back = cot_wide * gate_wide
        back_spec = jnp.fft.rfft(back, n=length_two, axis=1)
        spread = jnp.fft.irfft(back_spec * jnp.conj(tap_spec), n=length_two, axis=1)[:, :seq_len]
        corr = jnp.fft.irfft(back_spec * jnp.conj(sig_spec), n=length_two, axis=1)[:, :seq_len]
        mixed = conv + skip_col * sig_wide
        out_result = (gate_wide * mixed).astype(jnp.bfloat16)
        out_gate = (cot_wide * mixed).astype(jnp.bfloat16)
        out_signal = (skip_col * back + spread).astype(jnp.bfloat16)
        return (summed + corr, (out_result, out_gate, out_signal))
    initial = jnp.zeros((channels, seq_len), jnp.float32)
    summed, (result, d_gate, d_signal) = lax.scan(one_context, initial, (signal, gate, cotangent))
    inside = points[None, :] < lengths[:, None]
    filter_full = jnp.where(inside, summed / math.sqrt(seq_len * sequences), 0.0)
    holders = channels // C_DEV
    slot_pos, slot_chan, filled = slot_layout(owner, holders, CAP)
    tap_grad = jnp.zeros((holders * CAP, seq_len), jnp.float32).at[slot_pos].set(filter_full)
    return (result, d_gate, d_signal, tap_grad)
```

```python
import math

import numpy as np

import jax
import jax.numpy as jnp
import ml_dtypes
from jax import lax
from jax.experimental import pallas as pl
from jax.experimental.pallas import tpu as pltpu
from jax.sharding import PartitionSpec as P

LANES = 128
GROUP = 4
VMEM_LIMIT = 48 * 1024 * 1024


def embed_table(seq_total, features):
    bands = (features - 1) // 2
    points = np.arange(seq_total, dtype=np.int64)
    freq_ids = np.arange(1, bands + 1, dtype=np.int64)
    phase = (freq_ids[:, None] * points[None, :] % seq_total).astype(np.float32) * np.float32(
        2.0 * math.pi / seq_total
    )
    ramp = points.astype(np.float32)[None, :] / np.float32(seq_total)
    table = np.concatenate([ramp, np.cos(phase), np.sin(phase)], axis=0)
    return table.astype(ml_dtypes.bfloat16)


def sine(x):
    turns = jnp.round(x * (1.0 / math.pi))
    r = x - turns * 3.140625
    r = r - turns * 9.67502593994140625e-4
    r = r - turns * 1.509957990978376432e-7
    half = turns * 0.5
    sign = 1.0 - 4.0 * (half - jnp.floor(half))
    s = r * r
    p = -1.0 / 39916800.0
    p = p * s + 1.0 / 362880.0
    p = p * s - 1.0 / 5040.0
    p = p * s + 1.0 / 120.0
    p = p * s - 1.0 / 6.0
    return sign * (r + r * s * p)


def taps_body(emb_ref, w_in_ref, w_mid_ref, w_out_ref, rate_ref, scale_ref, len_ref, out_ref, *, seq_len, width):
    rows = w_out_ref.shape[0]
    out_ref[0:rows, :] = jnp.zeros((rows, LANES), jnp.float32)
    w_in = w_in_ref[...]
    w_mid = w_mid_ref[...]
    w_out = w_out_ref[...]
    for part in range(seq_len // width):
        emb = emb_ref[:, part * width : (part + 1) * width]
        one = sine(jnp.dot(w_in, emb, preferred_element_type=jnp.float32)).astype(jnp.bfloat16)
        two = sine(jnp.dot(w_mid, one, preferred_element_type=jnp.float32)).astype(jnp.bfloat16)
        net = jnp.dot(w_out, two, preferred_element_type=jnp.float32)
        point = part * width + lax.broadcasted_iota(jnp.int32, (rows, width), 1)
        decay = jnp.exp(-rate_ref[...] * point.astype(jnp.float32) / seq_len)
        value = jnp.where(point < len_ref[...], net * decay * scale_ref[...], 0.0)
        value = value.astype(jnp.bfloat16).astype(jnp.float32)
        for sub in range(width // LANES):
            block = part * (width // LANES) + sub + 1
            out_ref[block * rows : (block + 1) * rows, :] = value[:, sub * LANES : (sub + 1) * LANES]


def make_taps(emb, w_in, w_mid, w_out_rows, rate_rows, length_rows, seq_len):
    rows = w_out_rows.shape[0]
    blocks = seq_len // LANES
    body = lambda *refs: taps_body(*refs, seq_len=seq_len, width=512)
    return pl.pallas_call(
        body,
        out_shape=jax.ShapeDtypeStruct(((blocks + 1) * rows, LANES), jnp.float32),
        compiler_params=pltpu.CompilerParams(vmem_limit_bytes=VMEM_LIMIT),
        name="taps",
    )(
        emb,
        w_in,
        w_mid,
        w_out_rows,
        rate_rows[:, None],
        lax.rsqrt(length_rows.astype(jnp.float32))[:, None],
        length_rows[:, None],
    )


def convolve_body(
    len_ref, arr_ref, tap_ref, out_ref, grad_ref,
    wide, flipped, xbuf, bbuf, fbuf, y_wide, z_wide, f_wide, g_prev, *, norm
):
    blocks, pair, _ = arr_ref.shape
    rows = pair // 2
    f32 = jnp.float32
    b16 = jnp.bfloat16
    flip = (
        lax.broadcasted_iota(jnp.int32, (LANES, LANES), 0)
        + lax.broadcasted_iota(jnp.int32, (LANES, LANES), 1)
        == LANES - 1
    ).astype(f32).astype(b16)
    wide[...] = arr_ref[...].reshape(blocks * pair, LANES).astype(f32)
    flipped[...] = jnp.dot(
        arr_ref[...].reshape(blocks * pair, LANES), flip, preferred_element_type=f32
    )
    f_wide[...] = jnp.zeros(f_wide.shape, f32)
    zero = jnp.zeros((blocks, LANES), f32)
    xbuf[0:blocks, :] = zero
    bbuf[blocks : 2 * blocks, :] = zero
    fbuf[blocks : 2 * blocks, :] = zero
    lane = lax.broadcasted_iota(jnp.int32, (8, LANES), 1)
    sub = lax.broadcasted_iota(jnp.int32, (8, LANES), 0)
    build_key = jnp.where(lane >= sub, lane, lane + LANES)
    sum_key = lane + sub

    def channel(c, carry):
        length = len_ref[c]
        xbuf[blocks : 2 * blocks, :] = wide[pl.ds(c, blocks, stride=pair), :]
        bbuf[0:blocks, :] = wide[pl.ds(rows + c, blocks, stride=pair), :]
        fbuf[0:blocks, :] = flipped[pl.ds(rows + c, blocks, stride=pair), :]
        xt = flipped[pl.ds(c, blocks, stride=pair), :].T.astype(b16)
        steps = jnp.minimum((length + LANES - 1) // LANES + 1, blocks)
        groups = (steps + GROUP - 1) // GROUP

        def diagonal(upper, lower):
            total = None
            for a in range(LANES // 8):
                piece = jnp.where(sum_key >= LANES - 1 - 8 * a, upper[8 * a : 8 * a + 8, :], lower[8 * a : 8 * a + 8, :])
                if a:
                    piece = pltpu.roll(piece, 8 * a, 1)
                total = piece if total is None else total + piece
            total = pltpu.roll(total, 1, 1, stride=1, stride_axis=0)
            return jnp.sum(total, axis=0, keepdims=True)

        def put(k, value):
            spot = k * LANES + lax.broadcasted_iota(jnp.int32, (1, LANES), 1)
            f_wide[pl.ds((k + 1) * rows + c, 1), :] = jnp.where(spot < length, value * norm, 0.0)

        def group(g, acc):
            first = g * GROUP
            heads = []
            for j in range(-1, GROUP):
                row = tap_ref[pl.ds((first + j + 1) * rows + c, 1), :]
                heads.append(pltpu.roll(jnp.broadcast_to(row, (8, LANES)), 0, 1, stride=1, stride_axis=0))
            built = []
            left = []
            right = []
            for j in range(GROUP):
                for a in range(LANES // 8):
                    piece = jnp.where(build_key >= LANES - 8 * a, heads[j], heads[j + 1])
                    built.append(pltpu.roll(piece, 8 * a, 1) if a else piece)
                left.append(
                    jnp.concatenate(
                        [xbuf[pl.ds(blocks - first - j, blocks), :], fbuf[pl.ds(first + j, blocks), :]], axis=0
                    ).astype(b16)
                )
                right.append(bbuf[pl.ds(first + j, blocks), :].astype(b16))
            toeplitz = jnp.concatenate(built, axis=0).astype(b16)
            acc = acc + jnp.dot(jnp.concatenate(left, axis=1), toeplitz, preferred_element_type=f32)
            outer = jnp.dot(xt, jnp.concatenate(right, axis=1), preferred_element_type=f32)
            before = g_prev[...]
            for j in range(GROUP):
                now = outer[:, j * LANES : (j + 1) * LANES]
                put(first + j - 1, diagonal(before, now))
                before = now
            g_prev[...] = before
            return acc

        acc = lax.fori_loop(0, groups, group, jnp.zeros((2 * blocks, LANES), f32))

        @pl.when(groups * GROUP == blocks)
        def _():
            last = g_prev[...]
            put(blocks - 1, diagonal(last, jnp.zeros_like(last)))

        y_wide[pl.ds(c, blocks, stride=rows), :] = acc[0:blocks, :]
        z_wide[pl.ds(c, blocks, stride=rows), :] = acc[blocks:, :]
        return carry

    lax.fori_loop(0, rows, channel, 0)
    out_ref[:, 0:rows, :] = y_wide[...].astype(b16).reshape(blocks, rows, LANES)
    out_ref[:, rows:, :] = (
        jnp.dot(z_wide[...].astype(b16), flip, preferred_element_type=f32).astype(b16).reshape(blocks, rows, LANES)
    )
    grad_ref[...] = f_wide[rows:, :].reshape(blocks, rows, LANES)


def convolve(length_rows, arrived, taps, norm):
    blocks, pair, _ = arrived.shape
    rows = pair // 2
    body = lambda *refs: convolve_body(*refs, norm=norm)
    vm = pl.BlockSpec(memory_space=pltpu.VMEM)
    wide = lambda n: pltpu.VMEM((n, LANES), jnp.float32)
    return pl.pallas_call(
        body,
        in_specs=[pl.BlockSpec(memory_space=pltpu.SMEM), vm, vm],
        out_specs=(vm, vm),
        out_shape=(
            jax.ShapeDtypeStruct((blocks, pair, LANES), jnp.bfloat16),
            jax.ShapeDtypeStruct((blocks, rows, LANES), jnp.float32),
        ),
        scratch_shapes=[
            wide(blocks * pair),
            wide(blocks * pair),
            wide(2 * blocks),
            wide(2 * blocks),
            wide(2 * blocks),
            wide(blocks * rows),
            wide(blocks * rows),
            wide((blocks + 1) * rows),
            wide(LANES),
        ],
        compiler_params=pltpu.CompilerParams(vmem_limit_bytes=VMEM_LIMIT),
        name="convolve",
    )(length_rows, arrived, taps)


def pick_body(me_ref, owner_ref, all_ref, out_ref):
    holders, cols, rows, _ = all_ref.shape
    f32 = jnp.float32
    b16 = jnp.bfloat16
    mine = (owner_ref[...] == me_ref[0]).astype(f32)
    lines = mine.shape[0]
    above = lax.broadcasted_iota(jnp.int32, (LANES, LANES), 0) < lax.broadcasted_iota(
        jnp.int32, (LANES, LANES), 1
    )
    within = jnp.dot(mine.astype(b16), above.astype(f32).astype(b16), preferred_element_type=f32)
    counts = jnp.sum(mine, axis=1, keepdims=True)
    slots = out_ref.shape[0]
    slot_id = lax.broadcasted_iota(jnp.int32, (slots, LANES), 0).astype(f32)
    start = jnp.zeros((1, 1), f32)
    pieces = []
    for line in range(lines):
        rank = within[line : line + 1, :] + start
        hit = (slot_id == rank) & (mine[line : line + 1, :] > 0.5)
        pieces.append(hit.astype(f32).astype(b16))
        start = start + counts[line : line + 1, :]
    chosen = jnp.concatenate(pieces, axis=1)
    for col in range(cols):
        table = all_ref[:, col, :, :].reshape(holders * rows, LANES)
        out_ref[:, col * LANES : (col + 1) * LANES] = jnp.dot(chosen, table, preferred_element_type=f32)


def pick_rows(me, owner, everyone, slots):
    holders, cols, rows, _ = everyone.shape
    vm = pl.BlockSpec(memory_space=pltpu.VMEM)
    return pl.pallas_call(
        pick_body,
        in_specs=[pl.BlockSpec(memory_space=pltpu.SMEM), vm, vm],
        out_specs=vm,
        out_shape=jax.ShapeDtypeStruct((slots, cols * LANES), jnp.float32),
        compiler_params=pltpu.CompilerParams(vmem_limit_bytes=VMEM_LIMIT),
        name="pick",
    )(me, owner.reshape(-1, LANES), everyone)


def shards(signal, gate, cotangent, w_in, w_mid, w_out, rates, skip, lengths, owner):
    ctx_count = lax.axis_size("ctx")
    place = lax.axis_index("ctx")
    channels, local_len = signal.shape[1:]
    seq_len = local_len * ctx_count
    sequences = signal.shape[0] * lax.axis_size("dp")
    norm = 1.0 / math.sqrt(seq_len * sequences)
    rows = channels // ctx_count
    f32 = jnp.float32
    b16 = jnp.bfloat16

    sig, gat, cot = signal[0], gate[0], cotangent[0]
    back = cot.astype(f32) * gat.astype(f32)
    outgoing = jnp.concatenate(
        [sig.reshape(ctx_count, rows, local_len), back.astype(b16).reshape(ctx_count, rows, local_len)], axis=1
    )
    arrived = lax.all_to_all(outgoing, "ctx", split_axis=0, concat_axis=0, tiled=True)

    def own(array):
        return lax.dynamic_slice_in_dim(array, place * rows, rows, 0)

    features = w_in.shape[1]
    padded = -(-features // 16) * 16
    table = np.zeros((padded, seq_len), ml_dtypes.bfloat16)
    table[:features] = embed_table(seq_len, features)
    w_in_wide = jnp.pad(w_in, ((0, 0), (0, padded - features)))
    own_lengths = own(lengths)
    taps = make_taps(jnp.asarray(table), w_in_wide, w_mid, own(w_out), own(rates), own_lengths, seq_len)

    outs, grads = convolve(own_lengths, arrived, taps, norm)
    mine = lax.psum_scatter(grads, "dp", scatter_dimension=0, tiled=True)
    everyone = lax.all_gather(mine.astype(b16), "ctx", axis=0, tiled=False)
    returned = lax.all_to_all(outs, "ctx", split_axis=0, concat_axis=0, tiled=True)
    conv = returned[:, :rows, :].reshape(channels, local_len).astype(f32)
    spread = returned[:, rows:, :].reshape(channels, local_len).astype(f32)
    mixed = conv + skip[:, None] * sig.astype(f32)
    result = (gat.astype(f32) * mixed).astype(b16)
    d_gate = (cot.astype(f32) * mixed).astype(b16)
    d_signal = (skip[:, None] * back + spread).astype(b16)
    tap_grad = pick_rows(place.reshape(1).astype(jnp.int32), owner, everyone, 2 * rows)
    return (result[None], d_gate[None], d_signal[None], tap_grad)


def solution(mesh):
    data = P("dp", None, "ctx")
    return jax.shard_map(
        shards,
        mesh=mesh,
        in_specs=(data, data, data, P(), P(), P(), P(), P(), P(), P()),
        out_specs=(data, data, data, P("ctx", "dp")),
        check_vma=False,
    )
```

```python
import math

import numpy as np

import jax
import jax.numpy as jnp
import ml_dtypes
from jax import lax
from jax.experimental import pallas as pl
from jax.experimental.pallas import tpu as pltpu
from jax.sharding import PartitionSpec as P

LANES = 128
GROUP = 8
VMEM_LIMIT = 48 * 1024 * 1024
F32 = jnp.float32
B16 = jnp.bfloat16
PARAMS = pltpu.CompilerParams(vmem_limit_bytes=VMEM_LIMIT)
VM = pl.BlockSpec(memory_space=pltpu.VMEM)
SM = pl.BlockSpec(memory_space=pltpu.SMEM)


def iota(shape, axis):
    return lax.broadcasted_iota(jnp.int32, shape, axis)


def flip_matrix():
    return (iota((LANES, LANES), 0) + iota((LANES, LANES), 1) == LANES - 1).astype(F32).astype(B16)


def embed_table(seq_total, features):
    bands = (features - 1) // 2
    points = np.arange(seq_total, dtype=np.int64)
    freq_ids = np.arange(1, bands + 1, dtype=np.int64)
    phase = (freq_ids[:, None] * points[None, :] % seq_total).astype(np.float32) * np.float32(
        2.0 * math.pi / seq_total
    )
    ramp = points.astype(np.float32)[None, :] / np.float32(seq_total)
    table = np.concatenate([ramp, np.cos(phase), np.sin(phase)], axis=0)
    return table.astype(ml_dtypes.bfloat16)


def sine(x):
    turns = jnp.round(x * (1.0 / math.pi))
    r = x - turns * 3.140625
    r = r - turns * 9.67502593994140625e-4
    r = r - turns * 1.509957990978376432e-7
    half = turns * 0.5
    sign = 1.0 - 4.0 * (half - jnp.floor(half))
    s = r * r
    p = -1.0 / 39916800.0
    p = p * s + 1.0 / 362880.0
    p = p * s - 1.0 / 5040.0
    p = p * s + 1.0 / 120.0
    p = p * s - 1.0 / 6.0
    return sign * (r + r * s * p)


def pack_body(sig_ref, gate_ref, cot_ref, out_ref, wide):
    half = sig_ref.shape[0] // 2
    for part in range(2):
        rows = slice(part * half, (part + 1) * half)
        wide[pl.ds(part, half, stride=4), :] = sig_ref[rows, :].astype(F32)
        wide[pl.ds(2 + part, half, stride=4), :] = cot_ref[rows, :].astype(F32) * gate_ref[rows, :].astype(F32)
    out_ref[...] = wide[...].astype(B16)


def pack(sig, gate, cot):
    rows = 2 * sig.shape[0]
    return pl.pallas_call(
        pack_body,
        in_specs=[VM] * 3,
        out_specs=VM,
        out_shape=jax.ShapeDtypeStruct((rows, LANES), B16),
        scratch_shapes=[pltpu.VMEM((rows, LANES), F32)],
        compiler_params=PARAMS,
        name="pack",
    )(sig, gate, cot)


def tables_body(
    emb_ref, w_in_ref, w_mid_ref, w_out_ref, rate_ref, scale_ref, len_ref, ahead_ref, behind_ref, taps, turned
):
    seq_len = emb_ref.shape[1]
    width = 512
    blocks = seq_len // LANES
    channels = w_out_ref.shape[0]
    w_in = w_in_ref[...]
    w_mid = w_mid_ref[...]
    w_out = w_out_ref[...]
    flip = flip_matrix()
    zero = jnp.zeros((8, LANES), F32)
    taps[0:8, :] = zero
    turned[0:8, :] = zero
    for part in range(seq_len // width):
        emb = emb_ref[:, part * width : (part + 1) * width]
        one = sine(jnp.dot(w_in, emb, preferred_element_type=F32)).astype(B16)
        two = sine(jnp.dot(w_mid, one, preferred_element_type=F32)).astype(B16)
        net = jnp.dot(w_out, two, preferred_element_type=F32)
        point = part * width + iota((channels, width), 1)
        decay = jnp.exp(-rate_ref[...] * point.astype(F32) / seq_len)
        value = jnp.where(point < len_ref[...], net * decay * scale_ref[...], 0.0).astype(B16)
        for piece in range(width // LANES):
            block = part * (width // LANES) + piece + 1
            here = value[:, piece * LANES : (piece + 1) * LANES]
            taps[block * 8 : block * 8 + channels, :] = here.astype(F32)
            turned[block * 8 : block * 8 + channels, :] = jnp.dot(here, flip, preferred_element_type=F32)
    lane = iota((8, LANES), 1)
    sub = iota((8, LANES), 0)
    build_key = jnp.where(lane >= sub, lane, lane + LANES)

    def head(ref, row, shift):
        spread = jnp.broadcast_to(ref[row : row + 1, :], (8, LANES))
        return pltpu.roll(spread, shift, 1, stride=1, stride_axis=0)

    def fill(out_ref, spot, low, high):
        built = []
        for a in range(LANES // 8):
            piece = jnp.where(build_key >= LANES - 8 * a, low, high)
            built.append(pltpu.roll(piece, 8 * a, 1) if a else piece)
        out_ref[spot * LANES : (spot + 1) * LANES, :] = jnp.concatenate(built, axis=0).astype(B16)

    for c in range(2):
        low = head(taps, c, 0)
        back_low = head(turned, c, 1)
        for k in range(blocks):
            high = head(taps, (k + 1) * 8 + c, 0)
            back_high = head(turned, (k + 1) * 8 + c, 1)
            fill(ahead_ref, c * blocks + k, low, high)
            fill_behind(behind_ref, c * blocks + k, back_low, back_high, lane, sub)
            low = high
            back_low = back_high


def fill_behind(out_ref, spot, low, high, lane, sub):
    key = jnp.where(lane >= sub + 1, lane, lane + LANES)
    built = []
    for a in range(LANES // 8):
        piece = jnp.where(key >= LANES - 8 * a, high, low)
        built.append(pltpu.roll(piece, 8 * a, 1) if a else piece)
    out_ref[spot * LANES : (spot + 1) * LANES, :] = jnp.concatenate(built, axis=0).astype(B16)


def make_tables(emb, w_in, w_mid, w_out, rate, scale, length):
    blocks = emb.shape[1] // LANES
    shape = jax.ShapeDtypeStruct((2 * blocks * LANES, LANES), B16)
    scratch = pltpu.VMEM(((blocks + 1) * 8, LANES), F32)
    return pl.pallas_call(
        tables_body,
        in_specs=[VM] * 7,
        out_specs=(VM, VM),
        out_shape=(shape, shape),
        scratch_shapes=[scratch, scratch],
        compiler_params=PARAMS,
        name="tables",
    )(emb, w_in, w_mid, w_out, rate, scale, length)


def diagonal(upper, lower, key):
    total = None
    for a in range(LANES // 8):
        rows = slice(8 * a, 8 * a + 8)
        piece = upper[rows, :] if lower is None else lower[rows, :]
        if lower is None:
            piece = jnp.where(key >= LANES - 1 - 8 * a, piece, 0.0)
        else:
            piece = jnp.where(key >= LANES - 1 - 8 * a, upper[rows, :], piece)
        if a:
            piece = pltpu.roll(piece, 8 * a, 1)
        total = piece if total is None else total + piece
    total = pltpu.roll(total, 1, 1, stride=1, stride_axis=0)
    return jnp.sum(total, axis=0, keepdims=True)


def convolve_body(len_ref, arr_ref, ahead_ref, behind_ref, out_ref, wide, sig, back, y_acc, z_acc, lags, *, norm):
    peers = arr_ref.shape[0] // 4
    blocks = ahead_ref.shape[0] // (2 * LANES)
    batch = peers // blocks
    pad = (GROUP - 1) * batch
    flip = flip_matrix()
    key = iota((8, LANES), 0) + iota((8, LANES), 1)
    wide[0 : 4 * peers, :] = arr_ref[...].astype(F32)
    zero = jnp.zeros((pad, LANES), B16)
    lags_all = []
    for c in range(2):
        sig[c, 0:pad, :] = zero
        sig[c, pad : pad + peers, :] = wide[pl.ds(c, peers, stride=4), :].astype(B16)
        back[c, 0:peers, :] = wide[pl.ds(2 + c, peers, stride=4), :].astype(B16)
        back[c, peers : peers + pad, :] = zero
    for c in range(2):
        turned = lax.dot_general(
            flip, sig[c, pad : pad + peers, :], (((1,), (1,)), ((), ())), preferred_element_type=F32
        ).astype(B16)
        before = None
        for first in range(0, blocks, GROUP):
            rows = (blocks - first) * batch
            spots = slice((c * blocks + first) * LANES, (c * blocks + first + GROUP) * LANES)
            left = jnp.concatenate(
                [sig[c, pad - j * batch : pad - j * batch + rows, :] for j in range(GROUP)], axis=1
            )
            moved = jnp.concatenate(
                [back[c, (first + j) * batch : (first + j) * batch + rows, :] for j in range(GROUP)], axis=1
            )
            y = jnp.dot(left, ahead_ref[spots, :], preferred_element_type=F32)
            z = jnp.dot(moved, behind_ref[spots, :], preferred_element_type=F32)
            if first == 0:
                y_acc[c] = y
                z_acc[c] = z
            else:
                y_acc[c, first * batch :, :] += y
                z_acc[c, 0:rows, :] += z
            outer = jnp.dot(turned[:, 0:rows], moved, preferred_element_type=F32)
            for j in range(GROUP):
                now = outer[:, j * LANES : (j + 1) * LANES]
                if before is not None:
                    lags[c * blocks + first + j - 1 : c * blocks + first + j, :] = diagonal(before, now, key)
                before = now
        lags[c * blocks + blocks - 1 : c * blocks + blocks, :] = diagonal(before, None, key)
    point = iota((blocks, LANES), 0) * LANES + iota((blocks, LANES), 1)
    for c in range(2):
        wide[pl.ds(c, peers, stride=8), :] = y_acc[c]
        wide[pl.ds(2 + c, peers, stride=8), :] = z_acc[c]
        here = slice(c * blocks, (c + 1) * blocks)
        lags[here, :] = jnp.where(point < len_ref[c], lags[here, :] * norm, 0.0)
        for half in range(2):
            column = lags[pl.ds(c * blocks + half, batch, stride=2), :]
            wide[pl.ds(4 + 2 * c + half, peers, stride=8), :] = jnp.concatenate([column] * blocks, axis=0)
    out_ref[...] = wide[...].astype(B16)


def convolve(lengths, arrived, ahead, behind, norm):
    peers = arrived.shape[0] // 4
    blocks = ahead.shape[0] // (2 * LANES)
    pad = (GROUP - 1) * (peers // blocks)
    body = lambda *refs: convolve_body(*refs, norm=norm)
    return pl.pallas_call(
        body,
        in_specs=[SM, VM, VM, VM],
        out_specs=VM,
        out_shape=jax.ShapeDtypeStruct((8 * peers, LANES), B16),
        scratch_shapes=[
            pltpu.VMEM((8 * peers, LANES), F32),
            pltpu.VMEM((2, peers + pad, LANES), B16),
            pltpu.VMEM((2, peers + pad, LANES), B16),
            pltpu.VMEM((2, peers, LANES), F32),
            pltpu.VMEM((2, peers, LANES), F32),
            pltpu.VMEM((2 * blocks, LANES), F32),
        ],
        compiler_params=PARAMS,
        name="convolve",
    )(lengths, arrived, ahead, behind)


def finish_body(
    me_ref, ret_ref, sig_ref, gate_ref, cot_ref, skip_ref, owner_ref, result_ref, d_gate_ref, d_sig_ref, grad_ref, wide
):
    wide[...] = ret_ref[...].astype(F32)
    half = sig_ref.shape[0] // 2
    for part in range(2):
        rows = slice(part * half, (part + 1) * half)
        skip = skip_ref[rows, :]
        gate = gate_ref[rows, :].astype(F32)
        cot = cot_ref[rows, :].astype(F32)
        mixed = wide[pl.ds(part, half, stride=8), :] + skip * sig_ref[rows, :].astype(F32)
        result_ref[rows, :] = (gate * mixed).astype(B16)
        d_gate_ref[rows, :] = (cot * mixed).astype(B16)
        d_sig_ref[rows, :] = (skip * (cot * gate) + wide[pl.ds(2 + part, half, stride=8), :]).astype(B16)
    mine = (owner_ref[...] == me_ref[0]).astype(F32)
    lines = mine.shape[0]
    above = (iota((LANES, LANES), 0) < iota((LANES, LANES), 1)).astype(F32).astype(B16)
    within = jnp.dot(mine.astype(B16), above, preferred_element_type=F32)
    counts = jnp.sum(mine, axis=1, keepdims=True)
    slots = grad_ref.shape[0]
    slot_id = iota((slots, LANES), 0).astype(F32)
    start = jnp.zeros((1, 1), F32)
    pieces = []
    for line in range(lines):
        rank = within[line : line + 1, :] + start
        hit = jnp.where(slot_id == rank, mine[line : line + 1, :], 0.0)
        pieces.append(hit.astype(B16))
        start = start + counts[line : line + 1, :]
    chosen = jnp.concatenate(pieces, axis=1)
    for column in range(2):
        table = jnp.concatenate(
            [wide[pl.ds(4 + 2 * c + column, half, stride=8), :].astype(B16) for c in range(2)], axis=0
        )
        grad_ref[:, column * LANES : (column + 1) * LANES] = jnp.dot(chosen, table, preferred_element_type=F32)


def finish(me, returned, sig, gate, cot, skip, owner, slots):
    data = jax.ShapeDtypeStruct(sig.shape, B16)
    return pl.pallas_call(
        finish_body,
        in_specs=[SM] + [VM] * 6,
        out_specs=(VM,) * 4,
        out_shape=(data, data, data, jax.ShapeDtypeStruct((slots, 2 * LANES), F32)),
        scratch_shapes=[pltpu.VMEM(returned.shape, F32)],
        compiler_params=PARAMS,
        name="finish",
    )(me, returned, sig, gate, cot, skip[:, None], owner.reshape(-1, LANES))


def exchange(array):
    return lax.all_to_all(array, ("ctx", "dp"), split_axis=0, concat_axis=0, tiled=True)


def shards(signal, gate, cotangent, w_in, w_mid, w_out, rates, skip, lengths, owner):
    ctx_count = lax.axis_size("ctx")
    dp_count = lax.axis_size("dp")
    ctx_place = lax.axis_index("ctx")
    channels, local_len = signal.shape[1:]
    seq_len = local_len * ctx_count
    norm = 1.0 / math.sqrt(seq_len * dp_count)
    peers = ctx_count * dp_count
    place = ctx_place * dp_count + lax.axis_index("dp")

    sig, gat, cot = signal[0], gate[0], cotangent[0]
    packed = pack(sig, gat, cot)
    arrived = exchange(packed)

    def own(array):
        return lax.dynamic_slice_in_dim(array.reshape(2, peers, -1), place, 1, 1)[:, 0]

    def wide_rows(array):
        return jnp.pad(array, ((0, 6), (0, 0)))

    features = w_in.shape[1]
    padded = -(-features // 16) * 16
    table = np.zeros((padded, seq_len), ml_dtypes.bfloat16)
    table[:features] = embed_table(seq_len, features)
    w_in_wide = jnp.pad(w_in, ((0, 0), (0, padded - features)))
    own_lengths = own(lengths)
    ahead, behind = make_tables(
        jnp.asarray(table),
        w_in_wide,
        w_mid,
        wide_rows(own(w_out)),
        wide_rows(own(rates)),
        wide_rows(lax.rsqrt(own_lengths.astype(F32))),
        wide_rows(own_lengths),
    )
    outs = convolve(own_lengths[:, 0], arrived, ahead, behind, norm)
    returned = exchange(outs)
    result, d_gate, d_signal, tap_grad = finish(
        ctx_place.reshape(1).astype(jnp.int32), returned, sig, gat, cot, skip, owner, 2 * channels // ctx_count
    )
    return (result[None], d_gate[None], d_signal[None], tap_grad)


def solution(mesh):
    data = P("dp", None, "ctx")
    return jax.shard_map(
        shards,
        mesh=mesh,
        in_specs=(data, data, data, P(), P(), P(), P(), P(), P(), P()),
        out_specs=(data, data, data, P("ctx", "dp")),
        check_vma=False,
    )
```

```python
import math

import numpy as np

import jax
import jax.numpy as jnp
import ml_dtypes
from jax import lax
from jax.experimental import pallas as pl
from jax.experimental.pallas import tpu as pltpu
from jax.sharding import PartitionSpec as P

LANES = 128
GROUP = 8
PACK_PARTS = 4
VMEM_LIMIT = 16 * 1024 * 1024
F32 = jnp.float32
B16 = jnp.bfloat16
PARAMS = pltpu.CompilerParams(vmem_limit_bytes=VMEM_LIMIT)
VM = pl.BlockSpec(memory_space=pltpu.VMEM)
SM = pl.BlockSpec(memory_space=pltpu.SMEM)
HB = pl.BlockSpec(memory_space=pltpu.HBM)


def iota(shape, axis):
    return lax.broadcasted_iota(jnp.int32, shape, axis)


def flip_matrix():
    return (iota((LANES, LANES), 0) + iota((LANES, LANES), 1) == LANES - 1).astype(F32).astype(B16)


def embed_table(seq_total, features):
    bands = (features - 1) // 2
    points = np.arange(seq_total, dtype=np.int64)
    freq_ids = np.arange(1, bands + 1, dtype=np.int64)
    phase = (freq_ids[:, None] * points[None, :] % seq_total).astype(np.float32) * np.float32(
        2.0 * math.pi / seq_total
    )
    ramp = points.astype(np.float32)[None, :] / np.float32(seq_total)
    table = np.concatenate([ramp, np.cos(phase), np.sin(phase)], axis=0)
    return table.astype(ml_dtypes.bfloat16)


def sine(x):
    turns = jnp.round(x * (1.0 / math.pi))
    r = x - turns * 3.140625
    r = r - turns * 9.67502593994140625e-4
    r = r - turns * 1.509957990978376432e-7
    half = turns * 0.5
    sign = 1.0 - 4.0 * (half - jnp.floor(half))
    s = r * r
    p = -1.0 / 39916800.0
    p = p * s + 1.0 / 362880.0
    p = p * s - 1.0 / 5040.0
    p = p * s + 1.0 / 120.0
    p = p * s - 1.0 / 6.0
    return sign * (r + r * s * p)


def pack_body(sig_hbm, gate_hbm, cot_hbm, out_hbm, sig_in, gate_in, cot_in, wide, out, in_sem, out_sem):
    half = sig_in.shape[0] // 2
    step = half // PACK_PARTS
    pairs = ((sig_hbm, sig_in), (gate_hbm, gate_in), (cot_hbm, cot_in))

    def reads(part):
        copies = []
        for which, (src, dst) in enumerate(pairs):
            for side in range(2):
                rows = pl.ds(side * half + part * step, step)
                sem = in_sem.at[(part * 3 + which) * 2 + side]
                copies.append(pltpu.make_async_copy(src.at[rows, :], dst.at[rows, :], sem))
        return copies

    def write(part):
        rows = pl.ds(part * 4 * step, 4 * step)
        return pltpu.make_async_copy(out.at[rows, :], out_hbm.at[rows, :], out_sem.at[part])

    for part in range(PACK_PARTS):
        for copy in reads(part):
            copy.start()
    for part in range(PACK_PARTS):
        for copy in reads(part):
            copy.wait()
        for side in range(2):
            rows = slice(side * half + part * step, side * half + (part + 1) * step)
            first = part * 4 * step
            back = cot_in[rows, :].astype(F32) * gate_in[rows, :].astype(F32)
            wide[pl.ds(first + side, step, stride=4), :] = sig_in[rows, :].astype(F32)
            wide[pl.ds(first + 2 + side, step, stride=4), :] = back
        rows = slice(part * 4 * step, (part + 1) * 4 * step)
        out[rows, :] = wide[rows, :].astype(B16)
        write(part).start()
    for part in range(PACK_PARTS):
        write(part).wait()


def pack(sig, gate, cot):
    rows = 2 * sig.shape[0]
    held = pltpu.VMEM(sig.shape, B16)
    return pl.pallas_call(
        pack_body,
        in_specs=[HB] * 3,
        out_specs=HB,
        out_shape=jax.ShapeDtypeStruct((rows, LANES), B16),
        scratch_shapes=[
            held,
            held,
            held,
            pltpu.VMEM((rows, LANES), F32),
            pltpu.VMEM((rows, LANES), B16),
            pltpu.SemaphoreType.DMA((6 * PACK_PARTS,)),
            pltpu.SemaphoreType.DMA((PACK_PARTS,)),
        ],
        compiler_params=PARAMS,
        name="pack",
    )(*(pltpu.with_memory_space_constraint(array, pltpu.HBM) for array in (sig, gate, cot)))


def tables_body(
    emb_ref, w_in_ref, w_mid_ref, w_out_ref, rate_ref, scale_ref, len_ref, ahead_ref, taps
):
    seq_len = emb_ref.shape[1]
    width = 512
    blocks = seq_len // LANES
    channels = w_out_ref.shape[0]
    w_in = w_in_ref[...]
    w_mid = w_mid_ref[...]
    w_out = w_out_ref[...]
    taps[0:8, :] = jnp.zeros((8, LANES), F32)
    for part in range(seq_len // width):
        emb = emb_ref[:, part * width : (part + 1) * width]
        one = sine(jnp.dot(w_in, emb, preferred_element_type=F32)).astype(B16)
        two = sine(jnp.dot(w_mid, one, preferred_element_type=F32)).astype(B16)
        net = jnp.dot(w_out, two, preferred_element_type=F32)
        point = part * width + iota((channels, width), 1)
        decay = jnp.exp(-rate_ref[...] * point.astype(F32) / seq_len)
        value = jnp.where(point < len_ref[...], net * decay * scale_ref[...], 0.0).astype(B16)
        for piece in range(width // LANES):
            block = part * (width // LANES) + piece + 1
            here = value[:, piece * LANES : (piece + 1) * LANES]
            taps[block * 8 : block * 8 + channels, :] = here.astype(F32)
    lane = iota((8, LANES), 1)
    sub = iota((8, LANES), 0)
    build_key = jnp.where(lane >= sub, lane, lane + LANES)

    def head(row):
        spread = jnp.broadcast_to(taps[row : row + 1, :], (8, LANES))
        return pltpu.roll(spread, 0, 1, stride=1, stride_axis=0)

    def fill(spot, low, high):
        built = []
        for a in range(LANES // 8):
            piece = jnp.where(build_key >= LANES - 8 * a, low, high)
            built.append(pltpu.roll(piece, 8 * a, 1) if a else piece)
        ahead_ref[spot * LANES : (spot + 1) * LANES, :] = jnp.concatenate(built, axis=0).astype(B16)

    for c in range(2):
        low = head(0)
        for k in range(blocks):
            high = head((k + 1) * 8 + c)
            fill(c * blocks + k, low, high)
            low = high


def make_tables(emb, w_in, w_mid, w_out, rate, scale, length):
    blocks = emb.shape[1] // LANES
    shape = jax.ShapeDtypeStruct((2 * blocks * LANES, LANES), B16)
    scratch = pltpu.VMEM(((blocks + 1) * 8, LANES), F32)
    return pl.pallas_call(
        tables_body,
        in_specs=[VM] * 7,
        out_specs=VM,
        out_shape=shape,
        scratch_shapes=[scratch],
        compiler_params=PARAMS,
        name="tables",
    )(emb, w_in, w_mid, w_out, rate, scale, length)


def diagonal(upper, lower, key):
    total = None
    for a in range(LANES // 8):
        rows = slice(8 * a, 8 * a + 8)
        piece = upper[rows, :] if lower is None else lower[rows, :]
        if lower is None:
            piece = jnp.where(key >= LANES - 1 - 8 * a, piece, 0.0)
        else:
            piece = jnp.where(key >= LANES - 1 - 8 * a, upper[rows, :], piece)
        if a:
            piece = pltpu.roll(piece, 8 * a, 1)
        total = piece if total is None else total + piece
    total = pltpu.roll(total, 1, 1, stride=1, stride_axis=0)
    return jnp.sum(total, axis=0, keepdims=True)


def convolve_body(len_ref, arr_ref, ahead_ref, out_ref, wide, sig, back, y_acc, z_acc, lags, *, norm):
    peers = arr_ref.shape[0] // 4
    blocks = ahead_ref.shape[0] // (2 * LANES)
    batch = peers // blocks
    pad = (GROUP - 1) * batch
    flip = flip_matrix()
    key = iota((8, LANES), 0) + iota((8, LANES), 1)
    wide[0 : 4 * peers, :] = arr_ref[...].astype(F32)
    zero = jnp.zeros((pad, LANES), B16)
    lags_all = []
    for c in range(2):
        sig[c, 0:pad, :] = zero
        sig[c, pad : pad + peers, :] = wide[pl.ds(c, peers, stride=4), :].astype(B16)
        back[c, 0:peers, :] = wide[pl.ds(2 + c, peers, stride=4), :].astype(B16)
        back[c, peers : peers + pad, :] = zero
    for c in range(2):
        turned = lax.dot_general(
            flip, sig[c, pad : pad + peers, :], (((1,), (1,)), ((), ())), preferred_element_type=F32
        ).astype(B16)
        before = None
        for first in range(0, blocks, GROUP):
            rows = (blocks - first) * batch
            spots = slice((c * blocks + first) * LANES, (c * blocks + first + GROUP) * LANES)
            left = jnp.concatenate(
                [sig[c, pad - j * batch : pad - j * batch + rows, :] for j in range(GROUP)], axis=1
            )
            moved = jnp.concatenate(
                [back[c, (first + j) * batch : (first + j) * batch + rows, :] for j in range(GROUP)], axis=1
            )
            y = jnp.dot(left, ahead_ref[spots, :], preferred_element_type=F32)
            table = jnp.concatenate(
                [ahead_ref[spots.start + j * LANES : spots.start + (j + 1) * LANES, :] for j in range(GROUP)], axis=1
            )
            z = lax.dot_general(moved, table, (((1,), (1,)), ((), ())), preferred_element_type=F32)
            if first == 0:
                y_acc[c] = y
                z_acc[c] = z
            else:
                y_acc[c, first * batch :, :] += y
                z_acc[c, 0:rows, :] += z
            outer = jnp.dot(turned[:, 0:rows], moved, preferred_element_type=F32)
            for j in range(GROUP):
                now = outer[:, j * LANES : (j + 1) * LANES]
                if before is not None:
                    lags[c * blocks + first + j - 1 : c * blocks + first + j, :] = diagonal(before, now, key)
                before = now
        lags[c * blocks + blocks - 1 : c * blocks + blocks, :] = diagonal(before, None, key)
    point = iota((blocks, LANES), 0) * LANES + iota((blocks, LANES), 1)
    for c in range(2):
        wide[pl.ds(c, peers, stride=8), :] = y_acc[c]
        wide[pl.ds(2 + c, peers, stride=8), :] = z_acc[c]
        here = slice(c * blocks, (c + 1) * blocks)
        lags[here, :] = jnp.where(point < len_ref[c], lags[here, :] * norm, 0.0)
        for half in range(2):
            column = lags[pl.ds(c * blocks + half, batch, stride=2), :]
            wide[pl.ds(4 + 2 * c + half, peers, stride=8), :] = jnp.concatenate([column] * blocks, axis=0)
    out_ref[...] = wide[...].astype(B16)


def convolve(lengths, arrived, ahead, norm):
    peers = arrived.shape[0] // 4
    blocks = ahead.shape[0] // (2 * LANES)
    pad = (GROUP - 1) * (peers // blocks)
    body = lambda *refs: convolve_body(*refs, norm=norm)
    return pl.pallas_call(
        body,
        in_specs=[SM, VM, VM],
        out_specs=VM,
        out_shape=jax.ShapeDtypeStruct((8 * peers, LANES), B16),
        scratch_shapes=[
            pltpu.VMEM((8 * peers, LANES), F32),
            pltpu.VMEM((2, peers + pad, LANES), B16),
            pltpu.VMEM((2, peers + pad, LANES), B16),
            pltpu.VMEM((2, peers, LANES), F32),
            pltpu.VMEM((2, peers, LANES), F32),
            pltpu.VMEM((2 * blocks, LANES), F32),
        ],
        compiler_params=PARAMS,
        name="convolve",
    )(lengths, arrived, ahead)


def finish_body(
    me_ref, ret_ref, sig_ref, gate_ref, cot_ref, skip_ref, owner_ref, result_ref, d_gate_ref, d_sig_ref, grad_ref, wide
):
    wide[...] = ret_ref[...].astype(F32)
    half = sig_ref.shape[0] // 2
    for part in range(2):
        rows = slice(part * half, (part + 1) * half)
        skip = skip_ref[rows, :]
        gate = gate_ref[rows, :].astype(F32)
        cot = cot_ref[rows, :].astype(F32)
        mixed = wide[pl.ds(part, half, stride=8), :] + skip * sig_ref[rows, :].astype(F32)
        result_ref[rows, :] = (gate * mixed).astype(B16)
        d_gate_ref[rows, :] = (cot * mixed).astype(B16)
        d_sig_ref[rows, :] = (skip * (cot * gate) + wide[pl.ds(2 + part, half, stride=8), :]).astype(B16)
    mine = (owner_ref[...] == me_ref[0]).astype(F32)
    lines = mine.shape[0]
    above = (iota((LANES, LANES), 0) < iota((LANES, LANES), 1)).astype(F32).astype(B16)
    within = jnp.dot(mine.astype(B16), above, preferred_element_type=F32)
    counts = jnp.sum(mine, axis=1, keepdims=True)
    slots = grad_ref.shape[0]
    slot_id = iota((slots, LANES), 0).astype(F32)
    start = jnp.zeros((1, 1), F32)
    pieces = []
    for line in range(lines):
        rank = within[line : line + 1, :] + start
        hit = jnp.where(slot_id == rank, mine[line : line + 1, :], 0.0)
        pieces.append(hit.astype(B16))
        start = start + counts[line : line + 1, :]
    chosen = jnp.concatenate(pieces, axis=1)
    for column in range(2):
        table = jnp.concatenate(
            [wide[pl.ds(4 + 2 * c + column, half, stride=8), :].astype(B16) for c in range(2)], axis=0
        )
        grad_ref[:, column * LANES : (column + 1) * LANES] = jnp.dot(chosen, table, preferred_element_type=F32)


def finish(me, returned, sig, gate, cot, skip, owner, slots):
    data = jax.ShapeDtypeStruct(sig.shape, B16)
    return pl.pallas_call(
        finish_body,
        in_specs=[SM] + [VM] * 6,
        out_specs=(VM,) * 4,
        out_shape=(data, data, data, jax.ShapeDtypeStruct((slots, 2 * LANES), F32)),
        scratch_shapes=[pltpu.VMEM(returned.shape, F32)],
        compiler_params=PARAMS,
        name="finish",
    )(me, returned, sig, gate, cot, skip[:, None], owner.reshape(-1, LANES))


def exchange(array):
    return lax.all_to_all(array, ("ctx", "dp"), split_axis=0, concat_axis=0, tiled=True)


def shards(signal, gate, cotangent, w_in, w_mid, w_out, rates, skip, lengths, owner):
    ctx_count = lax.axis_size("ctx")
    dp_count = lax.axis_size("dp")
    ctx_place = lax.axis_index("ctx")
    channels, local_len = signal.shape[1:]
    seq_len = local_len * ctx_count
    norm = 1.0 / math.sqrt(seq_len * dp_count)
    peers = ctx_count * dp_count
    place = ctx_place * dp_count + lax.axis_index("dp")

    sig, gat, cot = signal[0], gate[0], cotangent[0]
    packed = pack(sig, gat, cot)
    arrived = exchange(packed)

    def own(array):
        return lax.dynamic_slice_in_dim(array.reshape(2, peers, -1), place, 1, 1)[:, 0]

    def wide_rows(array):
        return jnp.pad(array, ((0, 6), (0, 0)))

    features = w_in.shape[1]
    padded = -(-features // 16) * 16
    table = np.zeros((padded, seq_len), ml_dtypes.bfloat16)
    table[:features] = embed_table(seq_len, features)
    w_in_wide = jnp.pad(w_in, ((0, 0), (0, padded - features)))
    own_lengths = own(lengths)
    ahead = make_tables(
        jnp.asarray(table),
        w_in_wide,
        w_mid,
        wide_rows(own(w_out)),
        wide_rows(own(rates)),
        wide_rows(lax.rsqrt(own_lengths.astype(F32))),
        wide_rows(own_lengths),
    )
    outs = convolve(own_lengths[:, 0], arrived, ahead, norm)
    returned = exchange(outs)
    result, d_gate, d_signal, tap_grad = finish(
        ctx_place.reshape(1).astype(jnp.int32), returned, sig, gat, cot, skip, owner, 2 * channels // ctx_count
    )
    return (result[None], d_gate[None], d_signal[None], tap_grad)


def solution(mesh):
    data = P("dp", None, "ctx")
    return jax.shard_map(
        shards,
        mesh=mesh,
        in_specs=(data, data, data, P(), P(), P(), P(), P(), P(), P()),
        out_specs=(data, data, data, P("ctx", "dp")),
        check_vma=False,
    )
```

```python
import math

import numpy as np

import jax
import jax.numpy as jnp
import ml_dtypes
from jax import lax
from jax.experimental import pallas as pl
from jax.experimental.pallas import tpu as pltpu
from jax.sharding import PartitionSpec as P

LANES = 128
GROUP = 8
PACK_PARTS = 4
VMEM_LIMIT = 16 * 1024 * 1024
F32 = jnp.float32
B16 = jnp.bfloat16
PARAMS = pltpu.CompilerParams(vmem_limit_bytes=VMEM_LIMIT)
VM = pl.BlockSpec(memory_space=pltpu.VMEM)
SM = pl.BlockSpec(memory_space=pltpu.SMEM)
HB = pl.BlockSpec(memory_space=pltpu.HBM)


def far(*arrays):
    return [pltpu.with_memory_space_constraint(array, pltpu.HBM) for array in arrays]


def iota(shape, axis):
    return lax.broadcasted_iota(jnp.int32, shape, axis)


def flip_matrix():
    return (iota((LANES, LANES), 0) + iota((LANES, LANES), 1) == LANES - 1).astype(F32).astype(B16)


def embed_table(seq_total, features):
    bands = (features - 1) // 2
    points = np.arange(seq_total, dtype=np.int64)
    freq_ids = np.arange(1, bands + 1, dtype=np.int64)
    phase = (freq_ids[:, None] * points[None, :] % seq_total).astype(np.float32) * np.float32(
        2.0 * math.pi / seq_total
    )
    ramp = points.astype(np.float32)[None, :] / np.float32(seq_total)
    table = np.concatenate([ramp, np.cos(phase), np.sin(phase)], axis=0)
    return table.astype(ml_dtypes.bfloat16)


def sine(x):
    turns = jnp.round(x * (1.0 / math.pi))
    r = x - turns * 3.140625
    r = r - turns * 9.67502593994140625e-4
    r = r - turns * 1.509957990978376432e-7
    half = turns * 0.5
    sign = 1.0 - 4.0 * (half - jnp.floor(half))
    s = r * r
    p = -1.0 / 39916800.0
    p = p * s + 1.0 / 362880.0
    p = p * s - 1.0 / 5040.0
    p = p * s + 1.0 / 120.0
    p = p * s - 1.0 / 6.0
    return sign * (r + r * s * p)


def owner_order(owner, holders):
    above = (iota((LANES, LANES), 0) < iota((LANES, LANES), 1)).astype(F32).astype(B16)
    before = (iota((holders, holders), 1) < iota((holders, holders), 0)).astype(F32).astype(B16)
    holder = iota((holders, LANES), 0)
    marks = []
    ahead = []
    seen = jnp.zeros((holders, 1), F32)
    for line in range(owner.shape[0]):
        mark = (holder == owner[line : line + 1, :]).astype(F32)
        marks.append(mark)
        ahead.append(jnp.dot(mark.astype(B16), above, preferred_element_type=F32) + seen)
        seen = seen + jnp.sum(mark, axis=1, keepdims=True)
    total = jnp.broadcast_to(seen, (holders, LANES)).astype(B16)
    start = jnp.dot(before, total, preferred_element_type=F32)
    return [jnp.sum(m * (a + start), axis=0, keepdims=True) for m, a in zip(marks, ahead)]


def pack_body(
    owner_hbm, sig_hbm, gate_hbm, cot_hbm, out_hbm, spot_ref,
    owner_in, sig_in, gate_in, cot_in, wide, out, owner_sem, in_sem, out_sem, *, holders
):
    channels = sig_in.shape[0]
    half = channels // 2
    step = channels // PACK_PARTS
    pairs = ((sig_hbm, sig_in), (gate_hbm, gate_in), (cot_hbm, cot_in))

    def reads(part):
        rows = pl.ds(part * step, step)
        return [
            pltpu.make_async_copy(src.at[rows, :], dst.at[rows, :], in_sem.at[part * 3 + which])
            for which, (src, dst) in enumerate(pairs)
        ]

    def write(part):
        rows = pl.ds(part * 2 * step, 2 * step)
        return pltpu.make_async_copy(out.at[rows, :], out_hbm.at[rows, :], out_sem.at[part])

    owner_copy = pltpu.make_async_copy(owner_hbm, owner_in, owner_sem.at[0])
    owner_copy.start()
    for part in range(PACK_PARTS):
        for copy in reads(part):
            copy.start()
    owner_copy.wait()
    spots = owner_order(owner_in[...], holders)
    place = iota((channels, LANES), 0).astype(F32)
    lines = [jnp.where(place == spot, 1.0, 0.0).astype(B16) for spot in spots]
    for line, spot in enumerate(spots):
        spot_ref[line : line + 1, :] = spot
    spot_ref[len(spots) :, :] = owner_in[...].astype(F32)
    values = []
    for part in range(PACK_PARTS):
        for copy in reads(part):
            copy.wait()
        rows = slice(part * step, (part + 1) * step)
        back = (cot_in[rows, :].astype(F32) * gate_in[rows, :].astype(F32)).astype(B16)
        values.append(jnp.concatenate([sig_in[rows, :], back], axis=1))
    moved = jnp.dot(
        jnp.concatenate(lines, axis=1), jnp.concatenate(values, axis=0), preferred_element_type=F32
    )
    for side in range(2):
        rows = slice(side * half, (side + 1) * half)
        wide[pl.ds(side, half, stride=4), :] = moved[rows, 0:LANES]
        wide[pl.ds(2 + side, half, stride=4), :] = moved[rows, LANES:]
    for part in range(PACK_PARTS):
        rows = slice(part * 2 * step, (part + 1) * 2 * step)
        out[rows, :] = wide[rows, :].astype(B16)
        write(part).start()
    for part in range(PACK_PARTS):
        write(part).wait()


def pack(owner, sig, gate, cot, holders):
    rows = 2 * sig.shape[0]
    held = pltpu.VMEM(sig.shape, B16)
    lines = owner.shape[0]
    return pl.pallas_call(
        lambda *refs: pack_body(*refs, holders=holders),
        in_specs=[HB] * 4,
        out_specs=(HB, VM),
        out_shape=(jax.ShapeDtypeStruct((rows, LANES), B16), jax.ShapeDtypeStruct((2 * lines, LANES), F32)),
        scratch_shapes=[
            pltpu.VMEM(owner.shape, jnp.int32),
            held,
            held,
            held,
            pltpu.VMEM((rows, LANES), F32),
            pltpu.VMEM((rows, LANES), B16),
            pltpu.SemaphoreType.DMA((1,)),
            pltpu.SemaphoreType.DMA((3 * PACK_PARTS,)),
            pltpu.SemaphoreType.DMA((PACK_PARTS,)),
        ],
        compiler_params=PARAMS,
        name="pack",
    )(*far(owner, sig, gate, cot))


def tables_body(
    place_ref, emb_hbm, w_in_ref, w_mid_hbm, w_out_hbm, rate_hbm, len_hbm, spot_ref, ahead_ref, own_ref,
    emb_ref, w_mid_ref, w_out_ref, rate_ref, len_ref, taps, in_sem
):
    seq_len = emb_ref.shape[1]
    width = 512
    blocks = seq_len // LANES
    channels = w_out_ref.shape[1]
    lines = channels // LANES
    pairs = (
        (rate_hbm, rate_ref), (len_hbm, len_ref), (w_out_hbm, w_out_ref), (w_mid_hbm, w_mid_ref), (emb_hbm, emb_ref)
    )
    copies = [pltpu.make_async_copy(src, dst, in_sem.at[which]) for which, (src, dst) in enumerate(pairs)]
    for copy in copies:
        copy.start()
    for copy in copies:
        copy.wait()
    target = (iota((8, LANES), 0) * (channels // 2) + place_ref[0]).astype(F32)
    marks = [jnp.where(spot_ref[line : line + 1, :] == target, 1.0, 0.0) for line in range(lines)]

    def chosen(ref, first=0):
        total = 0.0
        for line in range(lines):
            total = total + marks[line] * ref[first + line : first + line + 1, :].astype(F32)
        return jnp.sum(total, axis=1, keepdims=True)

    rate = chosen(rate_ref)
    length = chosen(len_ref)
    own_ref[0:2, :] = jnp.broadcast_to(length[0:2, :], (2, LANES))
    own_ref[2:4, :] = jnp.broadcast_to(chosen(spot_ref, lines)[0:2, :], (2, LANES))
    own_ref[4:8, :] = jnp.zeros((4, LANES), F32)
    scale = lax.rsqrt(jnp.maximum(length, 1.0))
    w_in = w_in_ref[...]
    w_mid = w_mid_ref[...]
    w_out = lax.dot_general(
        jnp.concatenate(marks, axis=1).astype(B16), w_out_ref[...], (((1,), (1,)), ((), ())), preferred_element_type=F32
    ).astype(B16)
    taps[0:8, :] = jnp.zeros((8, LANES), F32)
    for part in range(seq_len // width):
        emb = emb_ref[:, part * width : (part + 1) * width]
        one = sine(jnp.dot(w_in, emb, preferred_element_type=F32)).astype(B16)
        two = sine(jnp.dot(w_mid, one, preferred_element_type=F32)).astype(B16)
        net = jnp.dot(w_out, two, preferred_element_type=F32)
        point = (part * width + iota((8, width), 1)).astype(F32)
        decay = jnp.exp(-rate * point / seq_len)
        value = jnp.where(point < length, net * decay * scale, 0.0).astype(B16)
        for piece in range(width // LANES):
            block = part * (width // LANES) + piece + 1
            here = value[:, piece * LANES : (piece + 1) * LANES]
            taps[block * 8 : block * 8 + 8, :] = here.astype(F32)
    lane = iota((8, LANES), 1)
    sub = iota((8, LANES), 0)
    build_key = jnp.where(lane >= sub, lane, lane + LANES)

    def head(row):
        spread = jnp.broadcast_to(taps[row : row + 1, :], (8, LANES))
        return pltpu.roll(spread, 0, 1, stride=1, stride_axis=0)

    def fill(spot, low, high):
        built = []
        for a in range(LANES // 8):
            piece = jnp.where(build_key >= LANES - 8 * a, low, high)
            built.append(pltpu.roll(piece, 8 * a, 1) if a else piece)
        ahead_ref[spot * LANES : (spot + 1) * LANES, :] = jnp.concatenate(built, axis=0).astype(B16)

    for c in range(2):
        low = head(0)
        for k in range(blocks):
            high = head((k + 1) * 8 + c)
            fill(c * blocks + k, low, high)
            low = high


def make_tables(place, emb, w_in, w_mid, w_out, rate, length, spots):
    blocks = emb.shape[1] // LANES
    rate = rate.reshape(-1, LANES)
    length = length.reshape(-1, LANES)
    w_out = w_out.T
    held = [pltpu.VMEM(array.shape, array.dtype) for array in (emb, w_mid, w_out, rate, length)]
    emb, w_mid, w_out, rate, length = far(emb, w_mid, w_out, rate, length)
    return pl.pallas_call(
        tables_body,
        in_specs=[SM, HB, VM, HB, HB, HB, HB, VM],
        out_specs=(VM, VM),
        out_shape=(
            jax.ShapeDtypeStruct((2 * blocks * LANES, LANES), B16),
            jax.ShapeDtypeStruct((8, LANES), F32),
        ),
        scratch_shapes=[*held, pltpu.VMEM(((blocks + 1) * 8, LANES), F32), pltpu.SemaphoreType.DMA((5,))],
        compiler_params=PARAMS,
        name="tables",
    )(place, emb, w_in, w_mid, w_out, rate, length, spots)


def diagonal(upper, lower, key):
    total = None
    for a in range(LANES // 8):
        rows = slice(8 * a, 8 * a + 8)
        piece = upper[rows, :] if lower is None else lower[rows, :]
        if lower is None:
            piece = jnp.where(key >= LANES - 1 - 8 * a, piece, 0.0)
        else:
            piece = jnp.where(key >= LANES - 1 - 8 * a, upper[rows, :], piece)
        if a:
            piece = pltpu.roll(piece, 8 * a, 1)
        total = piece if total is None else total + piece
    total = pltpu.roll(total, 1, 1, stride=1, stride_axis=0)
    return jnp.sum(total, axis=0, keepdims=True)


def convolve_body(
    own_ref, arr_ref, ahead_ref, out_hbm, done_ref, wide, sig, back, y_acc, z_acc, lags, out, out_sem, *, norm
):
    peers = arr_ref.shape[0] // 4
    blocks = ahead_ref.shape[0] // (2 * LANES)
    batch = peers // blocks
    pad = (GROUP - 1) * batch
    flip = flip_matrix()
    key = iota((8, LANES), 0) + iota((8, LANES), 1)
    wide[0 : 4 * peers, :] = arr_ref[...].astype(F32)
    zero = jnp.zeros((pad, LANES), B16)
    for c in range(2):
        sig[c, 0:pad, :] = zero
        sig[c, pad : pad + peers, :] = wide[pl.ds(c, peers, stride=4), :].astype(B16)
        back[c, 0:peers, :] = wide[pl.ds(2 + c, peers, stride=4), :].astype(B16)
        back[c, peers : peers + pad, :] = zero
    for c in range(2):
        turned = lax.dot_general(
            flip, sig[c, pad : pad + peers, :], (((1,), (1,)), ((), ())), preferred_element_type=F32
        ).astype(B16)
        before = None
        for first in range(0, blocks, GROUP):
            rows = (blocks - first) * batch
            spots = slice((c * blocks + first) * LANES, (c * blocks + first + GROUP) * LANES)
            left = jnp.concatenate(
                [sig[c, pad - j * batch : pad - j * batch + rows, :] for j in range(GROUP)], axis=1
            )
            moved = jnp.concatenate(
                [back[c, (first + j) * batch : (first + j) * batch + rows, :] for j in range(GROUP)], axis=1
            )
            y = jnp.dot(left, ahead_ref[spots, :], preferred_element_type=F32)
            table = jnp.concatenate(
                [ahead_ref[spots.start + j * LANES : spots.start + (j + 1) * LANES, :] for j in range(GROUP)], axis=1
            )
            z = lax.dot_general(moved, table, (((1,), (1,)), ((), ())), preferred_element_type=F32)
            if first == 0:
                y_acc[c] = y
                z_acc[c] = z
            else:
                y_acc[c, first * batch :, :] += y
                z_acc[c, 0:rows, :] += z
            outer = jnp.dot(turned[:, 0:rows], moved, preferred_element_type=F32)
            for j in range(GROUP):
                now = outer[:, j * LANES : (j + 1) * LANES]
                if before is not None:
                    lags[c * blocks + first + j - 1 : c * blocks + first + j, :] = diagonal(before, now, key)
                before = now
        lags[c * blocks + blocks - 1 : c * blocks + blocks, :] = diagonal(before, None, key)
    point = (iota((blocks, LANES), 0) * LANES + iota((blocks, LANES), 1)).astype(F32)
    holder = jnp.concatenate([jnp.full((batch, LANES), h, jnp.int32) for h in range(blocks)], axis=0).astype(F32)
    for c in range(2):
        wide[pl.ds(c, peers, stride=6), :] = y_acc[c]
        wide[pl.ds(2 + c, peers, stride=6), :] = z_acc[c]
        here = slice(c * blocks, (c + 1) * blocks)
        lags[here, :] = jnp.where(point < own_ref[c : c + 1, :], lags[here, :] * norm, 0.0)
    for half in range(2):
        total = jnp.zeros((peers, LANES), F32)
        for c in range(2):
            column = lags[pl.ds(c * blocks + half, batch, stride=2), :]
            column = jnp.concatenate([column] * blocks, axis=0)
            total = jnp.where(holder == own_ref[2 + c : 3 + c, :], column, total)
        wide[pl.ds(4 + half, peers, stride=6), :] = total
    step = 6 * peers // PACK_PARTS

    def write(part):
        rows = pl.ds(part * step, step)
        return pltpu.make_async_copy(out.at[rows, :], out_hbm.at[rows, :], out_sem.at[part])

    for part in range(PACK_PARTS):
        rows = slice(part * step, (part + 1) * step)
        out[rows, :] = wide[rows, :].astype(B16)
        write(part).start()
    done_ref[...] = own_ref[...]
    for part in range(PACK_PARTS):
        write(part).wait()


def convolve(own, arrived, ahead, norm):
    peers = arrived.shape[0] // 4
    blocks = ahead.shape[0] // (2 * LANES)
    pad = (GROUP - 1) * (peers // blocks)
    body = lambda *refs: convolve_body(*refs, norm=norm)
    return pl.pallas_call(
        body,
        in_specs=[VM, VM, VM],
        out_specs=(HB, VM),
        out_shape=(jax.ShapeDtypeStruct((6 * peers, LANES), B16), jax.ShapeDtypeStruct(own.shape, F32)),
        scratch_shapes=[
            pltpu.VMEM((6 * peers, LANES), F32),
            pltpu.VMEM((2, peers + pad, LANES), B16),
            pltpu.VMEM((2, peers + pad, LANES), B16),
            pltpu.VMEM((2, peers, LANES), F32),
            pltpu.VMEM((2, peers, LANES), F32),
            pltpu.VMEM((2 * blocks, LANES), F32),
            pltpu.VMEM((6 * peers, LANES), B16),
            pltpu.SemaphoreType.DMA((PACK_PARTS,)),
        ],
        compiler_params=PARAMS,
        name="convolve",
    )(own, arrived, ahead)


def route_body(
    after_ref, spot_ref, skip_ref, sig_hbm, gate_hbm, cot_hbm, out_ref, direct_ref, pulled_ref, gate_ref, cot_ref, sig_ref, in_sem
):
    pairs = ((sig_hbm, sig_ref), (gate_hbm, gate_ref), (cot_hbm, cot_ref))
    copies = [pltpu.make_async_copy(src, dst, in_sem.at[which]) for which, (src, dst) in enumerate(pairs)]
    for copy in copies:
        copy.start()

    def turned(ref, line):
        return jnp.broadcast_to(ref[line : line + 1, :], (LANES, LANES)).T

    for line in range(skip_ref.shape[0]):
        out_ref[line * LANES : (line + 1) * LANES, :] = turned(spot_ref, line)
    for copy in copies:
        copy.wait()
    for line in range(skip_ref.shape[0]):
        rows = slice(line * LANES, (line + 1) * LANES)
        skip = turned(skip_ref, line)
        direct_ref[rows, :] = skip * sig_ref[rows, :].astype(F32)
        pulled_ref[rows, :] = skip * (cot_ref[rows, :].astype(F32) * gate_ref[rows, :].astype(F32))


def route(after, spots, skip, sig, gate, cot):
    data = jax.ShapeDtypeStruct(sig.shape, B16)
    wide = jax.ShapeDtypeStruct(sig.shape, F32)
    return pl.pallas_call(
        route_body,
        in_specs=[VM] * 3 + [HB] * 3,
        out_specs=(VM,) * 5,
        out_shape=(wide, wide, wide, data, data),
        scratch_shapes=[pltpu.VMEM(sig.shape, B16), pltpu.SemaphoreType.DMA((3,))],
        compiler_params=PARAMS,
        name="route",
    )(after, spots, skip.reshape(-1, LANES), *far(sig, gate, cot))


def finish_body(
    me_ref, ret_ref, route_ref, direct_ref, pulled_ref, gate_ref, cot_ref, spot_ref,
    result_hbm, d_gate_hbm, d_sig_hbm, grad_ref, wide, result, d_gate, d_sig, out_sem
):
    wide[...] = ret_ref[...].astype(F32)
    channels = gate_ref.shape[0]
    half = channels // 2

    def take(row):
        return wide[pl.ds(row, half, stride=6), :].astype(B16)

    sides = [jnp.concatenate([take(c), take(2 + c)], axis=1) for c in range(2)]
    arrived = jnp.concatenate(sides, axis=0)
    step = channels // PACK_PARTS
    pairs = ((result, result_hbm), (d_gate, d_gate_hbm), (d_sig, d_sig_hbm))

    def writes(part):
        rows = pl.ds(part * step, step)
        return [
            pltpu.make_async_copy(src.at[rows, :], dst.at[rows, :], out_sem.at[part * 3 + which])
            for which, (src, dst) in enumerate(pairs)
        ]

    lane = iota((step, LANES), 1).astype(F32)
    for part in range(PACK_PARTS):
        rows = slice(part * step, (part + 1) * step)
        spot = route_ref[rows, :]
        lines = [jnp.where(lane + line * LANES == spot, 1.0, 0.0).astype(B16) for line in range(channels // LANES)]
        both = jnp.dot(jnp.concatenate(lines, axis=1), arrived, preferred_element_type=F32)
        mixed = both[:, 0:LANES] + direct_ref[rows, :]
        result[rows, :] = (gate_ref[rows, :].astype(F32) * mixed).astype(B16)
        d_gate[rows, :] = (cot_ref[rows, :].astype(F32) * mixed).astype(B16)
        d_sig[rows, :] = (pulled_ref[rows, :] + both[:, LANES:]).astype(B16)
        for copy in writes(part):
            copy.start()

    def tally(hits):
        lanes = jnp.sum(hits.astype(F32), axis=0, keepdims=True)
        return jnp.sum(lanes, axis=1, keepdims=True)

    slots = grad_ref.shape[0]
    owner = spot_ref[spot_ref.shape[0] // 2 :, :]
    me = me_ref[0].astype(F32)
    slot = iota((slots, half), 0).astype(F32)
    first = tally(owner < me)
    count = tally(owner == me)
    source = slot + first
    source = jnp.where(source >= half, source - half, source)
    chosen = jnp.where((iota((slots, half), 1).astype(F32) == source) & (slot < count), 1.0, 0.0).astype(B16)
    table = jnp.concatenate([take(4), take(5)], axis=1)
    grad_ref[...] = jnp.dot(chosen, table, preferred_element_type=F32)
    for part in range(PACK_PARTS):
        for copy in writes(part):
            copy.wait()


def finish(me, returned, routed, spots, slots):
    gate = routed[3]
    data = jax.ShapeDtypeStruct(gate.shape, B16)
    held = pltpu.VMEM(gate.shape, B16)
    return pl.pallas_call(
        finish_body,
        in_specs=[SM] + [VM] * 7,
        out_specs=(HB, HB, HB, VM),
        out_shape=(data, data, data, jax.ShapeDtypeStruct((slots, 2 * LANES), F32)),
        scratch_shapes=[
            pltpu.VMEM(returned.shape, F32),
            held,
            held,
            held,
            pltpu.SemaphoreType.DMA((3 * PACK_PARTS,)),
        ],
        compiler_params=PARAMS,
        name="finish",
    )(me, returned, *routed, spots)


def exchange(array, rows):
    parts = lax.all_to_all(
        array.reshape(-1, rows, LANES), ("ctx", "dp"), split_axis=0, concat_axis=0, tiled=True
    )
    return parts.reshape(array.shape)


def shards(signal, gate, cotangent, w_in, w_mid, w_out, rates, skip, lengths, owner):
    ctx_count = lax.axis_size("ctx")
    dp_count = lax.axis_size("dp")
    ctx_place = lax.axis_index("ctx")
    channels, local_len = signal.shape[1:]
    seq_len = local_len * ctx_count
    norm = 1.0 / math.sqrt(seq_len * dp_count)
    place = ctx_place * dp_count + lax.axis_index("dp")

    sig, gat, cot = signal[0], gate[0], cotangent[0]
    owner = owner.reshape(-1, LANES)
    packed, spots = pack(owner, sig, gat, cot, ctx_count)
    arrived = exchange(packed, 4)

    features = w_in.shape[1]
    padded = -(-features // 16) * 16
    table = np.zeros((padded, seq_len), ml_dtypes.bfloat16)
    table[:features] = embed_table(seq_len, features)
    w_in_wide = jnp.pad(w_in, ((0, 0), (0, padded - features)))
    ahead, own = make_tables(
        place.reshape(1).astype(jnp.int32), jnp.asarray(table), w_in_wide, w_mid, w_out, rates, lengths, spots
    )
    outs, done = convolve(own, arrived, ahead, norm)
    routed = route(done, spots, skip, sig, gat, cot)
    returned = exchange(outs, 2)
    result, d_gate, d_signal, tap_grad = finish(
        ctx_place.reshape(1).astype(jnp.int32), returned, routed, spots, 2 * channels // ctx_count
    )
    return (result[None], d_gate[None], d_signal[None], tap_grad)


def solution(mesh):
    data = P("dp", None, "ctx")
    return jax.shard_map(
        shards,
        mesh=mesh,
        in_specs=(data, data, data, P(), P(), P(), P(), P(), P(), P()),
        out_specs=(data, data, data, P("ctx", "dp")),
        check_vma=False,
    )
```

```python
import math

import numpy as np

import jax
import jax.numpy as jnp
import ml_dtypes
from jax import lax
from jax.experimental import pallas as pl
from jax.experimental.pallas import tpu as pltpu
from jax.sharding import PartitionSpec as P

LANES = 128
PACK_PARTS = 4
VMEM_LIMIT = 16 * 1024 * 1024
F32 = jnp.float32
B16 = jnp.bfloat16
PARAMS = pltpu.CompilerParams(vmem_limit_bytes=VMEM_LIMIT)
VM = pl.BlockSpec(memory_space=pltpu.VMEM)
SM = pl.BlockSpec(memory_space=pltpu.SMEM)
HB = pl.BlockSpec(memory_space=pltpu.HBM)


def far(*arrays):
    return [pltpu.with_memory_space_constraint(array, pltpu.HBM) for array in arrays]


def iota(shape, axis):
    return lax.broadcasted_iota(jnp.int32, shape, axis)


def flip_matrix():
    return (iota((LANES, LANES), 0) + iota((LANES, LANES), 1) == LANES - 1).astype(F32).astype(B16)


def embed_table(seq_total, features):
    bands = (features - 1) // 2
    points = np.arange(seq_total, dtype=np.int64)
    freq_ids = np.arange(1, bands + 1, dtype=np.int64)
    phase = (freq_ids[:, None] * points[None, :] % seq_total).astype(np.float32) * np.float32(
        2.0 * math.pi / seq_total
    )
    ramp = points.astype(np.float32)[None, :] / np.float32(seq_total)
    table = np.concatenate([ramp, np.cos(phase), np.sin(phase)], axis=0)
    return table.astype(ml_dtypes.bfloat16)


def sine(x):
    turns = jnp.round(x * (1.0 / math.pi))
    r = x - turns * 3.140625
    r = r - turns * 9.67502593994140625e-4
    r = r - turns * 1.509957990978376432e-7
    half = turns * 0.5
    sign = 1.0 - 4.0 * (half - jnp.floor(half))
    s = r * r
    p = -1.0 / 39916800.0
    p = p * s + 1.0 / 362880.0
    p = p * s - 1.0 / 5040.0
    p = p * s + 1.0 / 120.0
    p = p * s - 1.0 / 6.0
    return sign * (r + r * s * p)


def owner_order(owner, holders):
    above = (iota((LANES, LANES), 0) < iota((LANES, LANES), 1)).astype(F32).astype(B16)
    before = (iota((holders, holders), 1) < iota((holders, holders), 0)).astype(F32).astype(B16)
    holder = iota((holders, LANES), 0)
    marks = []
    ahead = []
    seen = jnp.zeros((holders, 1), F32)
    for line in range(owner.shape[0]):
        mark = (holder == owner[line : line + 1, :]).astype(F32)
        marks.append(mark)
        ahead.append(jnp.dot(mark.astype(B16), above, preferred_element_type=F32) + seen)
        seen = seen + jnp.sum(mark, axis=1, keepdims=True)
    total = jnp.broadcast_to(seen, (holders, LANES)).astype(B16)
    start = jnp.dot(before, total, preferred_element_type=F32)
    return [jnp.sum(m * (a + start), axis=0, keepdims=True) for m, a in zip(marks, ahead)]


def pack_body(
    owner_hbm, sig_hbm, gate_hbm, cot_hbm, out_hbm, spot_ref,
    owner_in, sig_in, gate_in, cot_in, wide, out, owner_sem, in_sem, out_sem, *, holders
):
    channels = sig_in.shape[0]
    half = channels // 2
    step = channels // PACK_PARTS
    pairs = ((sig_hbm, sig_in), (gate_hbm, gate_in), (cot_hbm, cot_in))

    def reads(part):
        rows = pl.ds(part * step, step)
        return [
            pltpu.make_async_copy(src.at[rows, :], dst.at[rows, :], in_sem.at[part * 3 + which])
            for which, (src, dst) in enumerate(pairs)
        ]

    def write(part):
        rows = pl.ds(part * 2 * step, 2 * step)
        return pltpu.make_async_copy(out.at[rows, :], out_hbm.at[rows, :], out_sem.at[part])

    owner_copy = pltpu.make_async_copy(owner_hbm, owner_in, owner_sem.at[0])
    owner_copy.start()
    for part in range(PACK_PARTS):
        for copy in reads(part):
            copy.start()
    owner_copy.wait()
    spots = owner_order(owner_in[...], holders)
    for line, spot in enumerate(spots):
        spot_ref[line : line + 1, :] = spot
    spot_ref[len(spots) :, :] = owner_in[...].astype(F32)
    values = []
    for part in range(PACK_PARTS):
        for copy in reads(part):
            copy.wait()
        rows = slice(part * step, (part + 1) * step)
        back = (cot_in[rows, :].astype(F32) * gate_in[rows, :].astype(F32)).astype(B16)
        values.append(jnp.concatenate([sig_in[rows, :], back], axis=1))
    values = jnp.concatenate(values, axis=0)
    few = step // 2
    for part in range(PACK_PARTS):
        place = iota((few, LANES), 0) + part * few
        place = jnp.concatenate([place, place + half], axis=0).astype(F32)
        lines = [jnp.where(place == spot, 1.0, 0.0).astype(B16) for spot in spots]
        moved = jnp.dot(jnp.concatenate(lines, axis=1), values, preferred_element_type=F32)
        for side in range(2):
            rows = slice(side * few, (side + 1) * few)
            wide[pl.ds(4 * few * part + side, few, stride=4), :] = moved[rows, 0:LANES]
            wide[pl.ds(4 * few * part + 2 + side, few, stride=4), :] = moved[rows, LANES:]
        rows = slice(part * 2 * step, (part + 1) * 2 * step)
        out[rows, :] = wide[rows, :].astype(B16)
        write(part).start()
    for part in range(PACK_PARTS):
        write(part).wait()


def pack(owner, sig, gate, cot, holders):
    rows = 2 * sig.shape[0]
    held = pltpu.VMEM(sig.shape, B16)
    lines = owner.shape[0]
    return pl.pallas_call(
        lambda *refs: pack_body(*refs, holders=holders),
        in_specs=[HB] * 4,
        out_specs=(HB, VM),
        out_shape=(jax.ShapeDtypeStruct((rows, LANES), B16), jax.ShapeDtypeStruct((2 * lines, LANES), F32)),
        scratch_shapes=[
            pltpu.VMEM(owner.shape, jnp.int32),
            held,
            held,
            held,
            pltpu.VMEM((rows, LANES), F32),
            pltpu.VMEM((rows, LANES), B16),
            pltpu.SemaphoreType.DMA((1,)),
            pltpu.SemaphoreType.DMA((3 * PACK_PARTS,)),
            pltpu.SemaphoreType.DMA((PACK_PARTS,)),
        ],
        compiler_params=PARAMS,
        name="pack",
    )(*far(owner, sig, gate, cot))


def tables_body(
    place_ref, emb_hbm, w_in_ref, w_mid_hbm, w_out_hbm, rate_hbm, len_hbm, spot_ref, ahead_ref, own_ref,
    emb_ref, w_mid_ref, w_out_ref, rate_ref, len_ref, taps, in_sem
):
    seq_len = emb_ref.shape[1]
    width = 512
    blocks = seq_len // LANES
    channels = w_out_ref.shape[1]
    lines = channels // LANES
    pairs = (
        (rate_hbm, rate_ref), (len_hbm, len_ref), (w_out_hbm, w_out_ref), (w_mid_hbm, w_mid_ref), (emb_hbm, emb_ref)
    )
    copies = [pltpu.make_async_copy(src, dst, in_sem.at[which]) for which, (src, dst) in enumerate(pairs)]
    for copy in copies:
        copy.start()
    for copy in copies:
        copy.wait()
    target = (iota((8, LANES), 0) * (channels // 2) + place_ref[0]).astype(F32)
    marks = [jnp.where(spot_ref[line : line + 1, :] == target, 1.0, 0.0) for line in range(lines)]

    def chosen(ref, first=0):
        total = 0.0
        for line in range(lines):
            total = total + marks[line] * ref[first + line : first + line + 1, :].astype(F32)
        return jnp.sum(total, axis=1, keepdims=True)

    rate = chosen(rate_ref)
    length = chosen(len_ref)
    own_ref[0:2, :] = jnp.broadcast_to(length[0:2, :], (2, LANES))
    own_ref[2:4, :] = jnp.broadcast_to(chosen(spot_ref, lines)[0:2, :], (2, LANES))
    own_ref[4:8, :] = jnp.zeros((4, LANES), F32)
    scale = lax.rsqrt(jnp.maximum(length, 1.0))
    w_in = w_in_ref[...]
    w_mid = w_mid_ref[...]
    w_out = lax.dot_general(
        jnp.concatenate(marks, axis=1).astype(B16), w_out_ref[...], (((1,), (1,)), ((), ())), preferred_element_type=F32
    ).astype(B16)
    taps[0:8, :] = jnp.zeros((8, LANES), F32)
    for part in range(seq_len // width):
        emb = emb_ref[:, part * width : (part + 1) * width]
        one = sine(jnp.dot(w_in, emb, preferred_element_type=F32)).astype(B16)
        two = sine(jnp.dot(w_mid, one, preferred_element_type=F32)).astype(B16)
        net = jnp.dot(w_out, two, preferred_element_type=F32)
        point = (part * width + iota((8, width), 1)).astype(F32)
        decay = jnp.exp(-rate * point / seq_len)
        value = jnp.where(point < length, net * decay * scale, 0.0).astype(B16)
        for piece in range(width // LANES):
            block = part * (width // LANES) + piece + 1
            here = value[:, piece * LANES : (piece + 1) * LANES]
            taps[block * 8 : block * 8 + 8, :] = here.astype(F32)
    lane = iota((8, LANES), 1)
    sub = iota((8, LANES), 0)
    build_key = jnp.where(lane >= sub, lane, lane + LANES)

    def head(row):
        spread = jnp.broadcast_to(taps[row : row + 1, :], (8, LANES))
        return pltpu.roll(spread, 0, 1, stride=1, stride_axis=0)

    def fill(spot, low, high):
        built = []
        for a in range(LANES // 8):
            piece = jnp.where(build_key >= LANES - 8 * a, low, high)
            built.append(pltpu.roll(piece, 8 * a, 1) if a else piece)
        ahead_ref[spot * LANES : (spot + 1) * LANES, :] = jnp.concatenate(built, axis=0).astype(B16)

    for c in range(2):
        low = head(0)
        for k in range(blocks):
            high = head((k + 1) * 8 + c)
            fill(c * blocks + k, low, high)
            low = high


def make_tables(place, emb, w_in, w_mid, w_out, rate, length, spots):
    blocks = emb.shape[1] // LANES
    rate = rate.reshape(-1, LANES)
    length = length.reshape(-1, LANES)
    w_out = w_out.T
    held = [pltpu.VMEM(array.shape, array.dtype) for array in (emb, w_mid, w_out, rate, length)]
    emb, w_mid, w_out, rate, length = far(emb, w_mid, w_out, rate, length)
    return pl.pallas_call(
        tables_body,
        in_specs=[SM, HB, VM, HB, HB, HB, HB, VM],
        out_specs=(VM, VM),
        out_shape=(
            jax.ShapeDtypeStruct((2 * blocks * LANES, LANES), B16),
            jax.ShapeDtypeStruct((8, LANES), F32),
        ),
        scratch_shapes=[*held, pltpu.VMEM(((blocks + 1) * 8, LANES), F32), pltpu.SemaphoreType.DMA((5,))],
        compiler_params=PARAMS,
        name="tables",
    )(place, emb, w_in, w_mid, w_out, rate, length, spots)


def diagonal(here, after, key):
    total = None
    for a in range(LANES // 8):
        rows = slice(8 * a, 8 * a + 8)
        late = 0.0 if after is None else after[rows, :]
        piece = jnp.where(key >= LANES - 8 * a, late, here[rows, :])
        if a:
            piece = pltpu.roll(piece, 8 * a, 1)
        total = piece if total is None else total + piece
    total = pltpu.roll(total, 0, 1, stride=1, stride_axis=0)
    return jnp.sum(total, axis=0, keepdims=True)


def convolve_body(own_ref, arr_ref, ahead_ref, out, wide, sig, back, lags, spread, *, norm):
    peers = arr_ref.shape[0] // 4
    blocks = ahead_ref.shape[0] // (2 * LANES)
    batch = peers // blocks
    pairs = blocks // 2
    count = pairs * batch
    pad = sig.shape[2] - count
    part = pairs // 2
    flip = flip_matrix()
    same = (iota((LANES, LANES), 0) == iota((LANES, LANES), 1)).astype(F32).astype(B16)
    key = iota((8, LANES), 0) + iota((8, LANES), 1)
    wide[...] = arr_ref[...].astype(F32)
    zero = jnp.zeros((pad, LANES), B16)
    empty = jnp.zeros((LANES, LANES), B16)

    for c in range(2):
        x = wide[pl.ds(c, peers, stride=4), :].astype(B16).reshape(pairs, 2, batch, LANES)
        b = jnp.dot(wide[pl.ds(2 + c, peers, stride=4), :].astype(B16), flip, preferred_element_type=F32)
        b = b.astype(B16).reshape(pairs, 2, batch, LANES)
        for e in range(2):
            sig[c, e, 0:pad, :] = zero
            sig[c, e, pad:, :] = x[:, e].reshape(count, LANES)
            back[c, e, 0:count, :] = b[:, e].reshape(count, LANES)
            back[c, e, count:, :] = zero

    def send(c, row, first, value):
        for i in range(value.shape[0] // batch):
            for e in range(2):
                peer = (2 * (first + i) + e) * batch
                spread[pl.ds(6 * peer + row + c, batch, stride=6), :] = value[
                    i * batch : (i + 1) * batch, e * LANES : (e + 1) * LANES
                ]

    for c in range(2):

        def table(k):
            spot = (c * blocks + k) * LANES
            return ahead_ref[spot : spot + LANES, :] if k >= 0 else empty

        def grid(*tables):
            rows = [jnp.concatenate([table(k) for k in line], axis=1) for line in tables]
            return jnp.concatenate(rows, axis=0)

        def earlier(first, m):
            rows = slice(pad + (first - m) * batch, pad + (first - m + part) * batch)
            return [sig[c, 0, rows, :], sig[c, 1, rows, :]]

        def later(first, m):
            rows = slice((first + m) * batch, (first + m + part) * batch)
            return [back[c, 0, rows, :], back[c, 1, rows, :]]

        turned = [
            lax.dot_general(same, sig[c, e, pad:, :], (((1,), (1,)), ((), ())), preferred_element_type=F32).astype(B16)
            for e in range(2)
        ]
        for first in range(0, pairs, part):
            deep = range(first + part)
            left = jnp.concatenate([piece for m in deep for piece in earlier(first, m)], axis=1)
            right = [grid((2 * m, 2 * m + 1), (2 * m - 1, 2 * m)) for m in deep]
            send(c, 0, first, jnp.dot(left, jnp.concatenate(right, axis=0), preferred_element_type=F32))
            deep = range(pairs - first)
            left = jnp.concatenate([piece for m in deep for piece in later(first, m)], axis=1)
            right = [grid((2 * m, 2 * m - 1), (2 * m + 1, 2 * m)) for m in deep]
            send(c, 2, first, jnp.dot(left, jnp.concatenate(right, axis=0), preferred_element_type=F32))
        before = None
        for first in range(0, pairs, 4):
            rows = count if first < part else count // 2
            upper = []
            lower = []
            for m in range(first, first + 4):
                here = slice(m * batch, m * batch + rows)
                next_ = slice((m + 1) * batch, (m + 1) * batch + rows)
                upper += [back[c, 0, here, :], back[c, 1, here, :]]
                lower += [back[c, 1, here, :], back[c, 0, next_, :]]
            right = jnp.concatenate([jnp.concatenate(upper, axis=1), jnp.concatenate(lower, axis=1)], axis=0)
            left = jnp.concatenate([side[:, 0:rows] for side in turned], axis=1)
            outer = jnp.dot(left, right, preferred_element_type=F32)
            for j in range(8):
                now = outer[:, j * LANES : (j + 1) * LANES]
                if before is not None:
                    spot = c * blocks + 2 * first + j - 1
                    lags[spot : spot + 1, :] = diagonal(before, now, key)
                before = now
        lags[(c + 1) * blocks - 1 : (c + 1) * blocks, :] = diagonal(before, None, key)
    point = (iota((blocks, LANES), 0) * LANES + iota((blocks, LANES), 1)).astype(F32)
    holder = jnp.concatenate([jnp.full((batch, LANES), h, jnp.int32) for h in range(blocks)], axis=0).astype(F32)
    ordered = jnp.dot((lags[...] * norm).astype(B16), flip, preferred_element_type=F32)
    for c in range(2):
        here = slice(c * blocks, (c + 1) * blocks)
        lags[here, :] = jnp.where(point < own_ref[c : c + 1, :], ordered[here, :], 0.0)
    for half in range(2):
        total = jnp.zeros((peers, LANES), F32)
        for c in range(2):
            column = lags[pl.ds(c * blocks + half, batch, stride=2), :]
            column = jnp.concatenate([column] * blocks, axis=0)
            total = jnp.where(holder == own_ref[2 + c : 3 + c, :], column, total)
        spread[pl.ds(4 + half, peers, stride=6), :] = total
    out[...] = spread[...].astype(B16)


def convolve(own, arrived, ahead, norm):
    peers = arrived.shape[0] // 4
    blocks = ahead.shape[0] // (2 * LANES)
    rows = peers // 2 + LANES
    body = lambda *refs: convolve_body(*refs, norm=norm)
    return pl.pallas_call(
        body,
        in_specs=[VM, VM, VM],
        out_specs=VM,
        out_shape=jax.ShapeDtypeStruct((6 * peers, LANES), B16),
        scratch_shapes=[
            pltpu.VMEM((4 * peers, LANES), F32),
            pltpu.VMEM((2, 2, rows, LANES), B16),
            pltpu.VMEM((2, 2, rows, LANES), B16),
            pltpu.VMEM((2 * blocks, LANES), F32),
            pltpu.VMEM((6 * peers, LANES), F32),
        ],
        compiler_params=PARAMS,
        name="convolve",
    )(own, arrived, ahead)


def finish_body(
    me_ref, ret_ref, sig_ref, gate_ref, cot_ref, skip_ref, spot_ref,
    result_hbm, d_gate_hbm, d_sig_hbm, grad_ref, wide, result, d_gate, d_sig, out_sem
):
    wide[...] = ret_ref[...].astype(F32)
    channels = gate_ref.shape[0]
    half = channels // 2

    def take(row):
        return wide[pl.ds(row, half, stride=6), :].astype(B16)

    flip = flip_matrix()

    def ordered(row):
        return jnp.dot(take(row), flip, preferred_element_type=F32).astype(B16)

    sides = [jnp.concatenate([take(c), ordered(2 + c)], axis=1) for c in range(2)]
    arrived = jnp.concatenate(sides, axis=0)
    step = channels // PACK_PARTS
    pairs = ((result, result_hbm), (d_gate, d_gate_hbm), (d_sig, d_sig_hbm))

    def writes(part):
        rows = pl.ds(part * step, step)
        return [
            pltpu.make_async_copy(src.at[rows, :], dst.at[rows, :], out_sem.at[part * 3 + which])
            for which, (src, dst) in enumerate(pairs)
        ]

    lane = iota((step, LANES), 1).astype(F32)

    def turned(ref, part):
        few = step // LANES
        lines = [jnp.broadcast_to(ref[part * few + i : part * few + i + 1, :], (LANES, LANES)).T for i in range(few)]
        return jnp.concatenate(lines, axis=0)

    for part in range(PACK_PARTS):
        rows = slice(part * step, (part + 1) * step)
        spot = turned(spot_ref, part)
        skip = turned(skip_ref, part)
        gate = gate_ref[rows, :].astype(F32)
        cot = cot_ref[rows, :].astype(F32)
        lines = [jnp.where(lane + line * LANES == spot, 1.0, 0.0).astype(B16) for line in range(channels // LANES)]
        both = jnp.dot(jnp.concatenate(lines, axis=1), arrived, preferred_element_type=F32)
        mixed = both[:, 0:LANES] + skip * sig_ref[rows, :].astype(F32)
        result[rows, :] = (gate * mixed).astype(B16)
        d_gate[rows, :] = (cot * mixed).astype(B16)
        d_sig[rows, :] = (skip * (cot * gate) + both[:, LANES:]).astype(B16)
        for copy in writes(part):
            copy.start()

    def tally(hits):
        lanes = jnp.sum(hits.astype(F32), axis=0, keepdims=True)
        return jnp.sum(lanes, axis=1, keepdims=True)

    slots = grad_ref.shape[0]
    owner = spot_ref[spot_ref.shape[0] // 2 :, :]
    me = me_ref[0].astype(F32)
    slot = iota((slots, half), 0).astype(F32)
    first = tally(owner < me)
    count = tally(owner == me)
    source = slot + first
    source = jnp.where(source >= half, source - half, source)
    chosen = jnp.where((iota((slots, half), 1).astype(F32) == source) & (slot < count), 1.0, 0.0).astype(B16)
    table = jnp.concatenate([take(4), take(5)], axis=1)
    grad_ref[...] = jnp.dot(chosen, table, preferred_element_type=F32)
    for part in range(PACK_PARTS):
        for copy in writes(part):
            copy.wait()


def finish(me, returned, sig, gate, cot, skip, spots, slots):
    data = jax.ShapeDtypeStruct(gate.shape, B16)
    held = pltpu.VMEM(gate.shape, B16)
    return pl.pallas_call(
        finish_body,
        in_specs=[SM] + [VM] * 6,
        out_specs=(HB, HB, HB, VM),
        out_shape=(data, data, data, jax.ShapeDtypeStruct((slots, 2 * LANES), F32)),
        scratch_shapes=[
            pltpu.VMEM(returned.shape, F32),
            held,
            held,
            held,
            pltpu.SemaphoreType.DMA((3 * PACK_PARTS,)),
        ],
        compiler_params=PARAMS,
        name="finish",
    )(me, returned, sig, gate, cot, skip.reshape(-1, LANES), spots)


def exchange(array, rows):
    parts = lax.all_to_all(
        array.reshape(-1, rows, LANES), ("ctx", "dp"), split_axis=0, concat_axis=0, tiled=True
    )
    return parts.reshape(array.shape)


def shards(signal, gate, cotangent, w_in, w_mid, w_out, rates, skip, lengths, owner):
    ctx_count = lax.axis_size("ctx")
    dp_count = lax.axis_size("dp")
    ctx_place = lax.axis_index("ctx")
    channels, local_len = signal.shape[1:]
    seq_len = local_len * ctx_count
    norm = 1.0 / math.sqrt(seq_len * dp_count)
    place = ctx_place * dp_count + lax.axis_index("dp")

    sig, gat, cot = signal[0], gate[0], cotangent[0]
    owner = owner.reshape(-1, LANES)
    packed, spots = pack(owner, sig, gat, cot, ctx_count)
    arrived = exchange(packed, 4)

    features = w_in.shape[1]
    padded = -(-features // 16) * 16
    table = np.zeros((padded, seq_len), ml_dtypes.bfloat16)
    table[:features] = embed_table(seq_len, features)
    w_in_wide = jnp.pad(w_in, ((0, 0), (0, padded - features)))
    ahead, own = make_tables(
        place.reshape(1).astype(jnp.int32), jnp.asarray(table), w_in_wide, w_mid, w_out, rates, lengths, spots
    )
    outs = convolve(own, arrived, ahead, norm)
    returned = exchange(outs, 2)
    result, d_gate, d_signal, tap_grad = finish(
        ctx_place.reshape(1).astype(jnp.int32), returned, sig, gat, cot, skip, spots, 2 * channels // ctx_count
    )
    return (result[None], d_gate[None], d_signal[None], tap_grad)


def solution(mesh):
    data = P("dp", None, "ctx")
    return jax.shard_map(
        shards,
        mesh=mesh,
        in_specs=(data, data, data, P(), P(), P(), P(), P(), P(), P()),
        out_specs=(data, data, data, P("ctx", "dp")),
        check_vma=False,
    )
```

```python
import math

import numpy as np

import jax
import jax.numpy as jnp
import ml_dtypes
from jax import lax
from jax.experimental import pallas as pl
from jax.experimental.pallas import tpu as pltpu
from jax.sharding import PartitionSpec as P

LANES = 128
PACK_PARTS = 4
VMEM_LIMIT = 16 * 1024 * 1024
F32 = jnp.float32
B16 = jnp.bfloat16
PARAMS = pltpu.CompilerParams(vmem_limit_bytes=VMEM_LIMIT)
VM = pl.BlockSpec(memory_space=pltpu.VMEM)
SM = pl.BlockSpec(memory_space=pltpu.SMEM)
HB = pl.BlockSpec(memory_space=pltpu.HBM)


def far(*arrays):
    return [pltpu.with_memory_space_constraint(array, pltpu.HBM) for array in arrays]


def iota(shape, axis):
    return lax.broadcasted_iota(jnp.int32, shape, axis)


def flip_matrix():
    return (iota((LANES, LANES), 0) + iota((LANES, LANES), 1) == LANES - 1).astype(F32).astype(B16)


def embed_table(seq_total, features):
    bands = (features - 1) // 2
    points = np.arange(seq_total, dtype=np.int64)
    freq_ids = np.arange(1, bands + 1, dtype=np.int64)
    phase = (freq_ids[:, None] * points[None, :] % seq_total).astype(np.float32) * np.float32(
        2.0 * math.pi / seq_total
    )
    ramp = points.astype(np.float32)[None, :] / np.float32(seq_total)
    table = np.concatenate([ramp, np.cos(phase), np.sin(phase)], axis=0)
    return table.astype(ml_dtypes.bfloat16)


def sine(x):
    turns = jnp.round(x * (1.0 / math.pi))
    r = x - turns * 3.140625
    r = r - turns * 9.67502593994140625e-4
    r = r - turns * 1.509957990978376432e-7
    half = turns * 0.5
    sign = 1.0 - 4.0 * (half - jnp.floor(half))
    s = r * r
    p = -1.0 / 39916800.0
    p = p * s + 1.0 / 362880.0
    p = p * s - 1.0 / 5040.0
    p = p * s + 1.0 / 120.0
    p = p * s - 1.0 / 6.0
    return sign * (r + r * s * p)


def owner_order(owner, holders):
    above = (iota((LANES, LANES), 0) < iota((LANES, LANES), 1)).astype(F32).astype(B16)
    before = (iota((holders, holders), 1) < iota((holders, holders), 0)).astype(F32).astype(B16)
    holder = iota((holders, LANES), 0)
    marks = []
    ahead = []
    seen = jnp.zeros((holders, 1), F32)
    for line in range(owner.shape[0]):
        mark = (holder == owner[line : line + 1, :]).astype(F32)
        marks.append(mark)
        ahead.append(jnp.dot(mark.astype(B16), above, preferred_element_type=F32) + seen)
        seen = seen + jnp.sum(mark, axis=1, keepdims=True)
    total = jnp.broadcast_to(seen, (holders, LANES)).astype(B16)
    start = jnp.dot(before, total, preferred_element_type=F32)
    return [jnp.sum(m * (a + start), axis=0, keepdims=True) for m, a in zip(marks, ahead)]


def pack_body(
    owner_hbm, sig_hbm, gate_hbm, cot_hbm, out_hbm, spot_ref,
    owner_in, sig_in, gate_in, cot_in, wide, out, owner_sem, in_sem, out_sem, *, holders
):
    channels = sig_in.shape[0]
    half = channels // 2
    step = channels // PACK_PARTS
    pairs = ((sig_hbm, sig_in), (gate_hbm, gate_in), (cot_hbm, cot_in))

    reads = [pltpu.make_async_copy(src, dst, in_sem.at[which]) for which, (src, dst) in enumerate(pairs)]

    def write(part):
        rows = pl.ds(part * 2 * step, 2 * step)
        return pltpu.make_async_copy(out.at[rows, :], out_hbm.at[rows, :], out_sem.at[part])

    owner_copy = pltpu.make_async_copy(owner_hbm, owner_in, owner_sem.at[0])
    owner_copy.start()
    for copy in reads:
        copy.start()
    owner_copy.wait()
    spots = owner_order(owner_in[...], holders)
    for line, spot in enumerate(spots):
        spot_ref[line : line + 1, :] = spot
    spot_ref[len(spots) :, :] = owner_in[...].astype(F32)
    for copy in reads:
        copy.wait()
    back = (cot_in[...].astype(F32) * gate_in[...].astype(F32)).astype(B16)
    values = jnp.concatenate([sig_in[...], back], axis=1)
    few = step // 2
    row = iota((LANES, LANES), 0).astype(F32).astype(B16)
    one = jnp.ones((LANES, LANES), B16)
    none = jnp.zeros((LANES, LANES), B16)

    def onehot(block, spot):
        low = spot - block * LANES
        low = jnp.where((low >= 0) & (low < LANES), low, 2.0 * LANES).astype(B16)
        return jnp.where(row == low, one, none)

    for part in range(PACK_PARTS):
        chosen = []
        for side in range(2):
            for block in range(few // LANES):
                block += (side * half + part * few) // LANES
                chosen.append(jnp.concatenate([onehot(block, spot) for spot in spots], axis=1))
        moved = jnp.dot(jnp.concatenate(chosen, axis=0), values, preferred_element_type=F32)
        for side in range(2):
            rows = slice(side * few, (side + 1) * few)
            wide[pl.ds(4 * few * part + side, few, stride=4), :] = moved[rows, 0:LANES]
            wide[pl.ds(4 * few * part + 2 + side, few, stride=4), :] = moved[rows, LANES:]
        rows = slice(part * 2 * step, (part + 1) * 2 * step)
        out[rows, :] = wide[rows, :].astype(B16)
        write(part).start()
    for part in range(PACK_PARTS):
        write(part).wait()


def pack(owner, sig, gate, cot, holders):
    rows = 2 * sig.shape[0]
    held = pltpu.VMEM(sig.shape, B16)
    lines = owner.shape[0]
    return pl.pallas_call(
        lambda *refs: pack_body(*refs, holders=holders),
        in_specs=[HB] * 4,
        out_specs=(HB, VM),
        out_shape=(jax.ShapeDtypeStruct((rows, LANES), B16), jax.ShapeDtypeStruct((2 * lines, LANES), F32)),
        scratch_shapes=[
            pltpu.VMEM(owner.shape, jnp.int32),
            held,
            held,
            held,
            pltpu.VMEM((rows, LANES), F32),
            pltpu.VMEM((rows, LANES), B16),
            pltpu.SemaphoreType.DMA((1,)),
            pltpu.SemaphoreType.DMA((3,)),
            pltpu.SemaphoreType.DMA((PACK_PARTS,)),
        ],
        compiler_params=PARAMS,
        name="pack",
    )(*far(owner, sig, gate, cot))


def tables_body(
    place_ref, emb_hbm, w_in_ref, w_mid_hbm, w_out_hbm, rate_hbm, len_hbm, spot_ref, ahead_ref, own_ref,
    emb_ref, w_mid_ref, w_out_ref, rate_ref, len_ref, taps, in_sem
):
    seq_len = emb_ref.shape[1]
    width = 512
    blocks = seq_len // LANES
    channels = w_out_ref.shape[1]
    lines = channels // LANES
    pairs = (
        (rate_hbm, rate_ref), (len_hbm, len_ref), (w_out_hbm, w_out_ref), (w_mid_hbm, w_mid_ref), (emb_hbm, emb_ref)
    )
    copies = [pltpu.make_async_copy(src, dst, in_sem.at[which]) for which, (src, dst) in enumerate(pairs)]
    for copy in copies:
        copy.start()
    for copy in copies:
        copy.wait()
    target = (iota((8, LANES), 0) * (channels // 2) + place_ref[0]).astype(F32)
    marks = [jnp.where(spot_ref[line : line + 1, :] == target, 1.0, 0.0) for line in range(lines)]

    def chosen(ref, first=0):
        total = 0.0
        for line in range(lines):
            total = total + marks[line] * ref[first + line : first + line + 1, :].astype(F32)
        return jnp.sum(total, axis=1, keepdims=True)

    rate = chosen(rate_ref)
    length = chosen(len_ref)
    own_ref[0:2, :] = jnp.broadcast_to(length[0:2, :], (2, LANES))
    own_ref[2:4, :] = jnp.broadcast_to(chosen(spot_ref, lines)[0:2, :], (2, LANES))
    own_ref[4:8, :] = jnp.full((4, LANES), place_ref[1], jnp.int32).astype(F32)
    scale = lax.rsqrt(jnp.maximum(length, 1.0))
    w_in = w_in_ref[...]
    w_mid = w_mid_ref[...]
    w_out = lax.dot_general(
        jnp.concatenate(marks, axis=1).astype(B16), w_out_ref[...], (((1,), (1,)), ((), ())), preferred_element_type=F32
    ).astype(B16)
    taps[0:8, :] = jnp.zeros((8, LANES), F32)
    for part in range(seq_len // width):
        emb = emb_ref[:, part * width : (part + 1) * width]
        one = sine(jnp.dot(w_in, emb, preferred_element_type=F32)).astype(B16)
        two = sine(jnp.dot(w_mid, one, preferred_element_type=F32)).astype(B16)
        net = jnp.dot(w_out, two, preferred_element_type=F32)
        point = (part * width + iota((8, width), 1)).astype(F32)
        decay = jnp.exp(-rate * point / seq_len)
        value = jnp.where(point < length, net * decay * scale, 0.0).astype(B16)
        for piece in range(width // LANES):
            block = part * (width // LANES) + piece + 1
            here = value[:, piece * LANES : (piece + 1) * LANES]
            taps[block * 8 : block * 8 + 8, :] = here.astype(F32)
    lane = iota((8, LANES), 1)
    sub = iota((8, LANES), 0)
    build_key = jnp.where(lane >= sub, lane, lane + LANES)

    def head(row):
        spread = jnp.broadcast_to(taps[row : row + 1, :], (8, LANES))
        return pltpu.roll(spread, 0, 1, stride=1, stride_axis=0)

    def fill(spot, low, high):
        built = []
        for a in range(LANES // 8):
            piece = jnp.where(build_key >= LANES - 8 * a, low, high)
            built.append(pltpu.roll(piece, 8 * a, 1) if a else piece)
        ahead_ref[spot * LANES : (spot + 1) * LANES, :] = jnp.concatenate(built, axis=0).astype(B16)

    for c in range(2):
        low = head(0)
        for k in range(blocks):
            high = head((k + 1) * 8 + c)
            fill(c * blocks + k, low, high)
            low = high


def make_tables(place, emb, w_in, w_mid, w_out, rate, length, spots):
    blocks = emb.shape[1] // LANES
    rate = rate.reshape(-1, LANES)
    length = length.reshape(-1, LANES)
    w_out = w_out.T
    held = [pltpu.VMEM(array.shape, array.dtype) for array in (emb, w_mid, w_out, rate, length)]
    emb, w_mid, w_out, rate, length = far(emb, w_mid, w_out, rate, length)
    return pl.pallas_call(
        tables_body,
        in_specs=[SM, HB, VM, HB, HB, HB, HB, VM],
        out_specs=(VM, VM),
        out_shape=(
            jax.ShapeDtypeStruct((2 * blocks * LANES, LANES), B16),
            jax.ShapeDtypeStruct((8, LANES), F32),
        ),
        scratch_shapes=[*held, pltpu.VMEM(((blocks + 1) * 8, LANES), F32), pltpu.SemaphoreType.DMA((5,))],
        compiler_params=PARAMS,
        name="tables",
    )(place, emb, w_in, w_mid, w_out, rate, length, spots)


def diagonal(here, after, key):
    total = None
    for a in range(LANES // 8):
        rows = slice(8 * a, 8 * a + 8)
        late = 0.0 if after is None else after[rows, :]
        piece = jnp.where(key >= LANES - 8 * a, late, here[rows, :])
        if a:
            piece = pltpu.roll(piece, 8 * a, 1)
        total = piece if total is None else total + piece
    total = pltpu.roll(total, 0, 1, stride=1, stride_axis=0)
    return jnp.sum(total, axis=0, keepdims=True)


def convolve_body(own_ref, arr_ref, ahead_ref, out, wide, sig, back, lags, spread, *, norm):
    peers = arr_ref.shape[0] // 4
    blocks = ahead_ref.shape[0] // (2 * LANES)
    batch = peers // blocks
    pairs = blocks // 2
    count = pairs * batch
    pad = sig.shape[2] - count
    part = pairs // 2
    flip = flip_matrix()
    same = (iota((LANES, LANES), 0) == iota((LANES, LANES), 1)).astype(F32).astype(B16)
    key = iota((8, LANES), 0) + iota((8, LANES), 1)
    wide[...] = arr_ref[...].astype(F32)
    zero = jnp.zeros((pad, LANES), B16)
    empty = jnp.zeros((LANES, LANES), B16)

    for c in range(2):
        x = wide[pl.ds(c, peers, stride=4), :].astype(B16).reshape(pairs, 2, batch, LANES)
        b = jnp.dot(wide[pl.ds(2 + c, peers, stride=4), :].astype(B16), flip, preferred_element_type=F32)
        b = b.astype(B16).reshape(pairs, 2, batch, LANES)
        for e in range(2):
            sig[c, e, 0:pad, :] = zero
            sig[c, e, pad:, :] = x[:, e].reshape(count, LANES)
            back[c, e, 0:count, :] = b[:, e].reshape(count, LANES)
            back[c, e, count:, :] = zero

    def send(c, row, first, value):
        for i in range(value.shape[0] // batch):
            for e in range(2):
                peer = (2 * (first + i) + e) * batch
                spread[pl.ds(6 * peer + row + c, batch, stride=6), :] = value[
                    i * batch : (i + 1) * batch, e * LANES : (e + 1) * LANES
                ]

    for c in range(2):

        def table(k):
            spot = (c * blocks + k) * LANES
            return ahead_ref[spot : spot + LANES, :] if k >= 0 else empty

        def grid(*tables):
            rows = [jnp.concatenate([table(k) for k in line], axis=1) for line in tables]
            return jnp.concatenate(rows, axis=0)

        def earlier(first, m):
            rows = slice(pad + (first - m) * batch, pad + (first - m + part) * batch)
            return [sig[c, 0, rows, :], sig[c, 1, rows, :]]

        def later(first, m):
            rows = slice((first + m) * batch, (first + m + part) * batch)
            return [back[c, 0, rows, :], back[c, 1, rows, :]]

        turned = [
            lax.dot_general(same, sig[c, e, pad:, :], (((1,), (1,)), ((), ())), preferred_element_type=F32).astype(B16)
            for e in range(2)
        ]
        for first in range(0, pairs, part):
            deep = range(first + part)
            left = jnp.concatenate([piece for m in deep for piece in earlier(first, m)], axis=1)
            right = [grid((2 * m, 2 * m + 1), (2 * m - 1, 2 * m)) for m in deep]
            send(c, 0, first, jnp.dot(left, jnp.concatenate(right, axis=0), preferred_element_type=F32))
            deep = range(pairs - first)
            left = jnp.concatenate([piece for m in deep for piece in later(first, m)], axis=1)
            right = [grid((2 * m, 2 * m - 1), (2 * m + 1, 2 * m)) for m in deep]
            send(c, 2, first, jnp.dot(left, jnp.concatenate(right, axis=0), preferred_element_type=F32))
        before = None
        for first in range(0, pairs, 4):
            rows = count if first < part else count // 2
            upper = []
            lower = []
            for m in range(first, first + 4):
                here = slice(m * batch, m * batch + rows)
                next_ = slice((m + 1) * batch, (m + 1) * batch + rows)
                upper += [back[c, 0, here, :], back[c, 1, here, :]]
                lower += [back[c, 1, here, :], back[c, 0, next_, :]]
            right = jnp.concatenate([jnp.concatenate(upper, axis=1), jnp.concatenate(lower, axis=1)], axis=0)
            left = jnp.concatenate([side[:, 0:rows] for side in turned], axis=1)
            outer = jnp.dot(left, right, preferred_element_type=F32)
            for j in range(8):
                now = outer[:, j * LANES : (j + 1) * LANES]
                if before is not None:
                    spot = c * blocks + 2 * first + j - 1
                    lags[spot : spot + 1, :] = diagonal(before, now, key)
                before = now
        lags[(c + 1) * blocks - 1 : (c + 1) * blocks, :] = diagonal(before, None, key)
    point = (iota((blocks, LANES), 0) * LANES + iota((blocks, LANES), 1)).astype(F32)
    holder = jnp.concatenate([jnp.full((batch, LANES), h, jnp.int32) for h in range(blocks)], axis=0).astype(F32)
    ordered = jnp.dot((lags[...] * norm).astype(B16), flip, preferred_element_type=F32)
    for c in range(2):
        here = slice(c * blocks, (c + 1) * blocks)
        lags[here, :] = jnp.where(point < own_ref[c : c + 1, :], ordered[here, :], 0.0)
    for half in range(2):
        total = jnp.zeros((peers, LANES), F32)
        for c in range(2):
            column = lags[pl.ds(c * blocks + half, batch, stride=2), :]
            column = jnp.concatenate([column] * blocks, axis=0)
            total = jnp.where(holder == own_ref[2 + c : 3 + c, :], column, total)
        spread[pl.ds(4 + half, peers, stride=6), :] = total
    out[...] = spread[...].astype(B16)


def convolve(own, arrived, ahead, norm):
    peers = arrived.shape[0] // 4
    blocks = ahead.shape[0] // (2 * LANES)
    rows = peers // 2 + LANES
    body = lambda *refs: convolve_body(*refs, norm=norm)
    return pl.pallas_call(
        body,
        in_specs=[VM, VM, VM],
        out_specs=VM,
        out_shape=jax.ShapeDtypeStruct((6 * peers, LANES), B16),
        scratch_shapes=[
            pltpu.VMEM((4 * peers, LANES), F32),
            pltpu.VMEM((2, 2, rows, LANES), B16),
            pltpu.VMEM((2, 2, rows, LANES), B16),
            pltpu.VMEM((2 * blocks, LANES), F32),
            pltpu.VMEM((6 * peers, LANES), F32),
        ],
        compiler_params=PARAMS,
        name="convolve",
    )(own, arrived, ahead)


def finish_body(
    own_ref, ret_ref, sig_ref, gate_ref, cot_ref, skip_ref, spot_ref,
    result_hbm, d_gate_hbm, d_sig_hbm, grad_hbm, wide, result, d_gate, d_sig, grad, out_sem, grad_sem
):
    wide[...] = ret_ref[...].astype(F32)
    channels = gate_ref.shape[0]
    half = channels // 2

    def take(row):
        return wide[pl.ds(row, half, stride=6), :].astype(B16)

    flip = flip_matrix()

    def ordered(row):
        return jnp.dot(take(row), flip, preferred_element_type=F32).astype(B16)

    sides = [jnp.concatenate([take(c), ordered(2 + c)], axis=1) for c in range(2)]
    arrived = jnp.concatenate(sides, axis=0)
    step = channels // PACK_PARTS
    pairs = ((result, result_hbm), (d_gate, d_gate_hbm), (d_sig, d_sig_hbm))

    def writes(part):
        rows = pl.ds(part * step, step)
        return [
            pltpu.make_async_copy(src.at[rows, :], dst.at[rows, :], out_sem.at[part * 3 + which])
            for which, (src, dst) in enumerate(pairs)
        ]

    def tally(hits):
        lanes = jnp.sum(hits.astype(F32), axis=0, keepdims=True)
        return jnp.sum(lanes, axis=1, keepdims=True)

    slots = grad.shape[0]
    owner = spot_ref[spot_ref.shape[0] // 2 :, :]
    me = own_ref[4:5, :]
    slot = iota((slots, half), 0).astype(F32)
    first = tally(owner < me)
    count = tally(owner == me)
    source = slot + first
    source = jnp.where(source >= half, source - half, source)
    chosen = jnp.where((iota((slots, half), 1).astype(F32) == source) & (slot < count), 1.0, 0.0).astype(B16)
    table = jnp.concatenate([take(4), take(5)], axis=1)
    grad[...] = jnp.dot(chosen, table, preferred_element_type=F32)
    grad_copy = pltpu.make_async_copy(grad, grad_hbm, grad_sem.at[0])
    grad_copy.start()
    lane = iota((step, LANES), 1).astype(F32)
    none = jnp.zeros((step, LANES), B16)

    def turned(ref, part):
        few = step // LANES
        lines = [jnp.broadcast_to(ref[part * few + i : part * few + i + 1, :], (LANES, LANES)).T for i in range(few)]
        return jnp.concatenate(lines, axis=0)

    for part in range(PACK_PARTS):
        rows = slice(part * step, (part + 1) * step)
        spot = turned(spot_ref, part)
        skip = turned(skip_ref, part)
        gate = gate_ref[rows, :].astype(F32)
        cot = cot_ref[rows, :].astype(F32)
        block = jnp.floor(spot * (1.0 / LANES))
        mark = jnp.where(lane == spot - block * LANES, 1.0, 0.0).astype(B16)
        block = block.astype(B16)
        lines = [jnp.where(block == line, mark, none) for line in range(channels // LANES)]
        both = jnp.dot(jnp.concatenate(lines, axis=1), arrived, preferred_element_type=F32)
        mixed = both[:, 0:LANES] + skip * sig_ref[rows, :].astype(F32)
        result[rows, :] = (gate * mixed).astype(B16)
        d_gate[rows, :] = (cot * mixed).astype(B16)
        d_sig[rows, :] = (skip * (cot * gate) + both[:, LANES:]).astype(B16)
        for copy in writes(part):
            copy.start()

    for part in range(PACK_PARTS):
        for copy in writes(part):
            copy.wait()
    grad_copy.wait()


def finish(own, returned, sig, gate, cot, skip, spots, slots):
    data = jax.ShapeDtypeStruct(gate.shape, B16)
    held = pltpu.VMEM(gate.shape, B16)
    return pl.pallas_call(
        finish_body,
        in_specs=[VM] * 7,
        out_specs=(HB,) * 4,
        out_shape=(data, data, data, jax.ShapeDtypeStruct((slots, 2 * LANES), F32)),
        scratch_shapes=[
            pltpu.VMEM(returned.shape, F32),
            held,
            held,
            held,
            pltpu.VMEM((slots, 2 * LANES), F32),
            pltpu.SemaphoreType.DMA((3 * PACK_PARTS,)),
            pltpu.SemaphoreType.DMA((1,)),
        ],
        compiler_params=PARAMS,
        name="finish",
    )(own, returned, sig, gate, cot, skip.reshape(-1, LANES), spots)


def exchange(array, rows):
    parts = lax.all_to_all(
        array.reshape(-1, rows, LANES), ("ctx", "dp"), split_axis=0, concat_axis=0, tiled=True
    )
    return parts.reshape(array.shape)


def shards(signal, gate, cotangent, w_in, w_mid, w_out, rates, skip, lengths, owner):
    ctx_count = lax.axis_size("ctx")
    dp_count = lax.axis_size("dp")
    ctx_place = lax.axis_index("ctx")
    channels, local_len = signal.shape[1:]
    seq_len = local_len * ctx_count
    norm = 1.0 / math.sqrt(seq_len * dp_count)
    place = ctx_place * dp_count + lax.axis_index("dp")

    sig, gat, cot = signal[0], gate[0], cotangent[0]
    owner = owner.reshape(-1, LANES)
    packed, spots = pack(owner, sig, gat, cot, ctx_count)
    arrived = exchange(packed, 4)

    features = w_in.shape[1]
    padded = -(-features // 16) * 16
    table = np.zeros((padded, seq_len), ml_dtypes.bfloat16)
    table[:features] = embed_table(seq_len, features)
    w_in_wide = jnp.pad(w_in, ((0, 0), (0, padded - features)))
    ahead, own = make_tables(
        jnp.stack([place, ctx_place]).astype(jnp.int32), jnp.asarray(table), w_in_wide, w_mid, w_out, rates, lengths, spots
    )
    outs = convolve(own, arrived, ahead, norm)
    returned = exchange(outs, 2)
    result, d_gate, d_signal, tap_grad = finish(
        own, returned, sig, gat, cot, skip, spots, 2 * channels // ctx_count
    )
    return (result[None], d_gate[None], d_signal[None], tap_grad)


def solution(mesh):
    data = P("dp", None, "ctx")
    return jax.shard_map(
        shards,
        mesh=mesh,
        in_specs=(data, data, data, P(), P(), P(), P(), P(), P(), P()),
        out_specs=(data, data, data, P("ctx", "dp")),
        check_vma=False,
    )
```

```python
import math

import numpy as np

import jax
import jax.numpy as jnp
import ml_dtypes
from jax import lax
from jax.experimental import pallas as pl
from jax.experimental.pallas import tpu as pltpu
from jax.sharding import PartitionSpec as P

LANES = 128
PACK_PARTS = 4
VMEM_LIMIT = 16 * 1024 * 1024
F32 = jnp.float32
B16 = jnp.bfloat16
PARAMS = pltpu.CompilerParams(vmem_limit_bytes=VMEM_LIMIT)
VM = pl.BlockSpec(memory_space=pltpu.VMEM)
SM = pl.BlockSpec(memory_space=pltpu.SMEM)
HB = pl.BlockSpec(memory_space=pltpu.HBM)


def far(*arrays):
    return [pltpu.with_memory_space_constraint(array, pltpu.HBM) for array in arrays]


def iota(shape, axis):
    return lax.broadcasted_iota(jnp.int32, shape, axis)


def flip_matrix():
    return (iota((LANES, LANES), 0) + iota((LANES, LANES), 1) == LANES - 1).astype(F32).astype(B16)


def embed_table(seq_total, features):
    bands = (features - 1) // 2
    points = np.arange(seq_total, dtype=np.int64)
    freq_ids = np.arange(1, bands + 1, dtype=np.int64)
    phase = (freq_ids[:, None] * points[None, :] % seq_total).astype(np.float32) * np.float32(
        2.0 * math.pi / seq_total
    )
    ramp = points.astype(np.float32)[None, :] / np.float32(seq_total)
    table = np.concatenate([ramp, np.cos(phase), np.sin(phase)], axis=0)
    return table.astype(ml_dtypes.bfloat16)


def sine(x):
    turns = jnp.round(x * (1.0 / math.pi))
    r = x - turns * 3.140625
    r = r - turns * 9.67502593994140625e-4
    r = r - turns * 1.509957990978376432e-7
    half = turns * 0.5
    sign = 1.0 - 4.0 * (half - jnp.floor(half))
    s = r * r
    p = -1.0 / 39916800.0
    p = p * s + 1.0 / 362880.0
    p = p * s - 1.0 / 5040.0
    p = p * s + 1.0 / 120.0
    p = p * s - 1.0 / 6.0
    return sign * (r + r * s * p)


def owner_order(owner, holders):
    above = (iota((LANES, LANES), 0) < iota((LANES, LANES), 1)).astype(F32).astype(B16)
    before = (iota((holders, holders), 1) < iota((holders, holders), 0)).astype(F32).astype(B16)
    holder = iota((holders, LANES), 0)
    marks = []
    ahead = []
    seen = jnp.zeros((holders, 1), F32)
    for line in range(owner.shape[0]):
        mark = (holder == owner[line : line + 1, :]).astype(F32)
        marks.append(mark)
        ahead.append(jnp.dot(mark.astype(B16), above, preferred_element_type=F32) + seen)
        seen = seen + jnp.sum(mark, axis=1, keepdims=True)
    total = jnp.broadcast_to(seen, (holders, LANES)).astype(B16)
    start = jnp.dot(before, total, preferred_element_type=F32)
    return [jnp.sum(m * (a + start), axis=0, keepdims=True) for m, a in zip(marks, ahead)]


def pack_body(
    owner_hbm, sig_hbm, gate_hbm, cot_hbm, out_hbm, spot_ref,
    owner_in, sig_in, gate_in, cot_in, wide, out, owner_sem, in_sem, out_sem, *, holders
):
    channels = sig_in.shape[0]
    half = channels // 2
    step = channels // PACK_PARTS
    pairs = ((sig_hbm, sig_in), (gate_hbm, gate_in), (cot_hbm, cot_in))

    reads = [pltpu.make_async_copy(src, dst, in_sem.at[which]) for which, (src, dst) in enumerate(pairs)]

    def write(part):
        rows = pl.ds(part * 2 * step, 2 * step)
        return pltpu.make_async_copy(out.at[rows, :], out_hbm.at[rows, :], out_sem.at[part])

    owner_copy = pltpu.make_async_copy(owner_hbm, owner_in, owner_sem.at[0])
    owner_copy.start()
    for copy in reads:
        copy.start()
    owner_copy.wait()
    spots = owner_order(owner_in[...], holders)
    for line, spot in enumerate(spots):
        spot_ref[line : line + 1, :] = spot
    spot_ref[len(spots) :, :] = owner_in[...].astype(F32)
    for copy in reads:
        copy.wait()
    back = (cot_in[...].astype(F32) * gate_in[...].astype(F32)).astype(B16)
    values = jnp.concatenate([sig_in[...], back], axis=1)
    few = step // 2
    row = iota((LANES, LANES), 0).astype(F32).astype(B16)
    one = jnp.ones((LANES, LANES), B16)
    none = jnp.zeros((LANES, LANES), B16)

    def onehot(block, spot):
        low = spot - block * LANES
        low = jnp.where((low >= 0) & (low < LANES), low, 2.0 * LANES).astype(B16)
        return jnp.where(row == low, one, none)

    for part in range(PACK_PARTS):
        chosen = []
        for side in range(2):
            for block in range(few // LANES):
                block += (side * half + part * few) // LANES
                chosen.append(jnp.concatenate([onehot(block, spot) for spot in spots], axis=1))
        moved = jnp.dot(jnp.concatenate(chosen, axis=0), values, preferred_element_type=F32)
        for side in range(2):
            rows = slice(side * few, (side + 1) * few)
            wide[pl.ds(4 * few * part + side, few, stride=4), :] = moved[rows, 0:LANES]
            wide[pl.ds(4 * few * part + 2 + side, few, stride=4), :] = moved[rows, LANES:]
        rows = slice(part * 2 * step, (part + 1) * 2 * step)
        out[rows, :] = wide[rows, :].astype(B16)
        write(part).start()
    for part in range(PACK_PARTS):
        write(part).wait()


def pack(owner, sig, gate, cot, holders):
    rows = 2 * sig.shape[0]
    held = pltpu.VMEM(sig.shape, B16)
    lines = owner.shape[0]
    return pl.pallas_call(
        lambda *refs: pack_body(*refs, holders=holders),
        in_specs=[HB] * 4,
        out_specs=(HB, VM),
        out_shape=(jax.ShapeDtypeStruct((rows, LANES), B16), jax.ShapeDtypeStruct((2 * lines, LANES), F32)),
        scratch_shapes=[
            pltpu.VMEM(owner.shape, jnp.int32),
            held,
            held,
            held,
            pltpu.VMEM((rows, LANES), F32),
            pltpu.VMEM((rows, LANES), B16),
            pltpu.SemaphoreType.DMA((1,)),
            pltpu.SemaphoreType.DMA((3,)),
            pltpu.SemaphoreType.DMA((PACK_PARTS,)),
        ],
        compiler_params=PARAMS,
        name="pack",
    )(*far(owner, sig, gate, cot))


def tables_body(
    place_ref, emb_hbm, w_in_ref, w_mid_hbm, w_out_hbm, rate_hbm, len_hbm, spot_ref, ahead_ref, own_ref,
    emb_ref, w_mid_ref, w_out_ref, rate_ref, len_ref, taps, in_sem
):
    seq_len = emb_ref.shape[1]
    width = 512
    blocks = seq_len // LANES
    channels = w_out_ref.shape[1]
    lines = channels // LANES
    pairs = (
        (rate_hbm, rate_ref), (len_hbm, len_ref), (w_out_hbm, w_out_ref), (w_mid_hbm, w_mid_ref), (emb_hbm, emb_ref)
    )
    copies = [pltpu.make_async_copy(src, dst, in_sem.at[which]) for which, (src, dst) in enumerate(pairs)]
    for copy in copies:
        copy.start()
    for copy in copies:
        copy.wait()
    target = (iota((8, LANES), 0) * (channels // 2) + place_ref[0]).astype(F32)
    marks = [jnp.where(spot_ref[line : line + 1, :] == target, 1.0, 0.0) for line in range(lines)]

    def chosen(ref, first=0):
        total = 0.0
        for line in range(lines):
            total = total + marks[line] * ref[first + line : first + line + 1, :].astype(F32)
        return jnp.sum(total, axis=1, keepdims=True)

    rate = chosen(rate_ref)
    length = chosen(len_ref)
    own_ref[0:2, :] = jnp.broadcast_to(length[0:2, :], (2, LANES))
    own_ref[2:4, :] = jnp.broadcast_to(chosen(spot_ref, lines)[0:2, :], (2, LANES))
    own_ref[4:8, :] = jnp.full((4, LANES), place_ref[1], jnp.int32).astype(F32)
    scale = lax.rsqrt(jnp.maximum(length, 1.0))
    w_in = w_in_ref[...]
    w_mid = w_mid_ref[...]
    w_out = lax.dot_general(
        jnp.concatenate(marks, axis=1).astype(B16), w_out_ref[...], (((1,), (1,)), ((), ())), preferred_element_type=F32
    ).astype(B16)
    taps[0:8, :] = jnp.zeros((8, LANES), F32)
    for part in range(seq_len // width):
        emb = emb_ref[:, part * width : (part + 1) * width]
        one = sine(jnp.dot(w_in, emb, preferred_element_type=F32)).astype(B16)
        two = sine(jnp.dot(w_mid, one, preferred_element_type=F32)).astype(B16)
        net = jnp.dot(w_out, two, preferred_element_type=F32)
        point = (part * width + iota((8, width), 1)).astype(F32)
        decay = jnp.exp(-rate * point / seq_len)
        value = jnp.where(point < length, net * decay * scale, 0.0).astype(B16)
        for piece in range(width // LANES):
            block = part * (width // LANES) + piece + 1
            here = value[:, piece * LANES : (piece + 1) * LANES]
            taps[block * 8 : block * 8 + 8, :] = here.astype(F32)
    lane = iota((8, LANES), 1)
    sub = iota((8, LANES), 0)
    build_key = jnp.where(lane >= sub, lane, lane + LANES)

    def head(row):
        spread = jnp.broadcast_to(taps[row : row + 1, :], (8, LANES))
        return pltpu.roll(spread, 0, 1, stride=1, stride_axis=0)

    def fill(spot, low, high):
        built = []
        for a in range(LANES // 8):
            piece = jnp.where(build_key >= LANES - 8 * a, low, high)
            built.append(pltpu.roll(piece, 8 * a, 1) if a else piece)
        ahead_ref[spot * LANES : (spot + 1) * LANES, :] = jnp.concatenate(built, axis=0).astype(B16)

    for c in range(2):
        low = head(0)
        for k in range(blocks):
            high = head((k + 1) * 8 + c)
            fill(c * blocks + k, low, high)
            low = high


def make_tables(place, emb, w_in, w_mid, w_out, rate, length, spots):
    blocks = emb.shape[1] // LANES
    rate = rate.reshape(-1, LANES)
    length = length.reshape(-1, LANES)
    w_out = w_out.T
    held = [pltpu.VMEM(array.shape, array.dtype) for array in (emb, w_mid, w_out, rate, length)]
    emb, w_mid, w_out, rate, length = far(emb, w_mid, w_out, rate, length)
    return pl.pallas_call(
        tables_body,
        in_specs=[SM, HB, VM, HB, HB, HB, HB, VM],
        out_specs=(VM, VM),
        out_shape=(
            jax.ShapeDtypeStruct((2 * blocks * LANES, LANES), B16),
            jax.ShapeDtypeStruct((8, LANES), F32),
        ),
        scratch_shapes=[*held, pltpu.VMEM(((blocks + 1) * 8, LANES), F32), pltpu.SemaphoreType.DMA((5,))],
        compiler_params=PARAMS,
        name="tables",
    )(place, emb, w_in, w_mid, w_out, rate, length, spots)


def diagonal(here, after, key):
    total = None
    for a in range(LANES // 8):
        rows = slice(8 * a, 8 * a + 8)
        late = 0.0 if after is None else after[rows, :]
        piece = jnp.where(key >= LANES - 8 * a, late, here[rows, :])
        if a:
            piece = pltpu.roll(piece, 8 * a, 1)
        total = piece if total is None else total + piece
    total = pltpu.roll(total, 0, 1, stride=1, stride_axis=0)
    return jnp.sum(total, axis=0, keepdims=True)


def convolve_body(own_ref, arr_ref, ahead_ref, out, wide, sig, back, lags, spread, *, norm):
    peers = arr_ref.shape[0] // 4
    blocks = ahead_ref.shape[0] // (2 * LANES)
    batch = peers // blocks
    pairs = blocks // 2
    count = pairs * batch
    pad = sig.shape[2] - count
    part = pairs // 2
    flip = flip_matrix()
    same = (iota((LANES, LANES), 0) == iota((LANES, LANES), 1)).astype(F32).astype(B16)
    key = iota((8, LANES), 0) + iota((8, LANES), 1)
    wide[...] = arr_ref[...].astype(F32)
    zero = jnp.zeros((pad, LANES), B16)
    empty = jnp.zeros((LANES, LANES), B16)

    for c in range(2):
        x = wide[pl.ds(c, peers, stride=4), :].astype(B16).reshape(pairs, 2, batch, LANES)
        b = jnp.dot(wide[pl.ds(2 + c, peers, stride=4), :].astype(B16), flip, preferred_element_type=F32)
        b = b.astype(B16).reshape(pairs, 2, batch, LANES)
        for e in range(2):
            sig[c, e, 0:pad, :] = zero
            sig[c, e, pad:, :] = x[:, e].reshape(count, LANES)
            back[c, e, 0:count, :] = b[:, e].reshape(count, LANES)
            back[c, e, count:, :] = zero

    def send(c, row, first, value):
        for i in range(value.shape[0] // batch):
            for e in range(2):
                peer = (2 * (first + i) + e) * batch
                spread[pl.ds(6 * peer + row + c, batch, stride=6), :] = value[
                    i * batch : (i + 1) * batch, e * LANES : (e + 1) * LANES
                ]

    for c in range(2):

        def table(k):
            spot = (c * blocks + k) * LANES
            return ahead_ref[spot : spot + LANES, :] if k >= 0 else empty

        def grid(*tables):
            rows = [jnp.concatenate([table(k) for k in line], axis=1) for line in tables]
            return jnp.concatenate(rows, axis=0)

        def earlier(first, m):
            rows = slice(pad + (first - m) * batch, pad + (first - m + part) * batch)
            return [sig[c, 0, rows, :], sig[c, 1, rows, :]]

        def later(first, m):
            rows = slice((first + m) * batch, (first + m + part) * batch)
            return [back[c, 0, rows, :], back[c, 1, rows, :]]

        turned = [
            lax.dot_general(same, sig[c, e, pad:, :], (((1,), (1,)), ((), ())), preferred_element_type=F32).astype(B16)
            for e in range(2)
        ]
        before = None
        for first in range(0, pairs, 4):
            rows = count if first < part else count // 2
            upper = []
            lower = []
            for m in range(first, first + 4):
                here = slice(m * batch, m * batch + rows)
                next_ = slice((m + 1) * batch, (m + 1) * batch + rows)
                upper += [back[c, 0, here, :], back[c, 1, here, :]]
                lower += [back[c, 1, here, :], back[c, 0, next_, :]]
            right = jnp.concatenate([jnp.concatenate(upper, axis=1), jnp.concatenate(lower, axis=1)], axis=0)
            left = jnp.concatenate([side[:, 0:rows] for side in turned], axis=1)
            outer = jnp.dot(left, right, preferred_element_type=F32)
            for j in range(8):
                now = outer[:, j * LANES : (j + 1) * LANES]
                if before is not None:
                    spot = c * blocks + 2 * first + j - 1
                    lags[spot : spot + 1, :] = diagonal(before, now, key)
                before = now
        lags[(c + 1) * blocks - 1 : (c + 1) * blocks, :] = diagonal(before, None, key)
        for first in range(0, pairs, part):
            deep = range(first + part)
            left = jnp.concatenate([piece for m in deep for piece in earlier(first, m)], axis=1)
            right = [grid((2 * m, 2 * m + 1), (2 * m - 1, 2 * m)) for m in deep]
            send(c, 0, first, jnp.dot(left, jnp.concatenate(right, axis=0), preferred_element_type=F32))
            deep = range(pairs - first)
            left = jnp.concatenate([piece for m in deep for piece in later(first, m)], axis=1)
            right = [grid((2 * m, 2 * m - 1), (2 * m + 1, 2 * m)) for m in deep]
            send(c, 2, first, jnp.dot(left, jnp.concatenate(right, axis=0), preferred_element_type=F32))
    point = (iota((blocks, LANES), 0) * LANES + iota((blocks, LANES), 1)).astype(F32)
    holder = jnp.concatenate([jnp.full((batch, LANES), h, jnp.int32) for h in range(blocks)], axis=0).astype(F32)
    ordered = jnp.dot((lags[...] * norm).astype(B16), flip, preferred_element_type=F32)
    for c in range(2):
        here = slice(c * blocks, (c + 1) * blocks)
        lags[here, :] = jnp.where(point < own_ref[c : c + 1, :], ordered[here, :], 0.0)
    for half in range(2):
        total = jnp.zeros((peers, LANES), F32)
        for c in range(2):
            column = lags[pl.ds(c * blocks + half, batch, stride=2), :]
            column = jnp.concatenate([column] * blocks, axis=0)
            total = jnp.where(holder == own_ref[2 + c : 3 + c, :], column, total)
        spread[pl.ds(4 + half, peers, stride=6), :] = total
    out[...] = spread[...].astype(B16)


def convolve(own, arrived, ahead, norm):
    peers = arrived.shape[0] // 4
    blocks = ahead.shape[0] // (2 * LANES)
    rows = peers // 2 + LANES
    body = lambda *refs: convolve_body(*refs, norm=norm)
    return pl.pallas_call(
        body,
        in_specs=[VM, VM, VM],
        out_specs=VM,
        out_shape=jax.ShapeDtypeStruct((6 * peers, LANES), B16),
        scratch_shapes=[
            pltpu.VMEM((4 * peers, LANES), F32),
            pltpu.VMEM((2, 2, rows, LANES), B16),
            pltpu.VMEM((2, 2, rows, LANES), B16),
            pltpu.VMEM((2 * blocks, LANES), F32),
            pltpu.VMEM((6 * peers, LANES), F32),
        ],
        compiler_params=PARAMS,
        name="convolve",
    )(own, arrived, ahead)


def finish_body(
    own_ref, ret_ref, sig_ref, gate_ref, cot_ref, skip_ref, spot_ref,
    result_hbm, d_gate_hbm, d_sig_hbm, grad_hbm, wide, result, d_gate, d_sig, grad, out_sem, grad_sem
):
    wide[...] = ret_ref[...].astype(F32)
    channels = gate_ref.shape[0]
    half = channels // 2

    def take(row):
        return wide[pl.ds(row, half, stride=6), :].astype(B16)

    flip = flip_matrix()

    def ordered(row):
        return jnp.dot(take(row), flip, preferred_element_type=F32).astype(B16)

    sides = [jnp.concatenate([take(c), ordered(2 + c)], axis=1) for c in range(2)]
    arrived = jnp.concatenate(sides, axis=0)
    step = channels // PACK_PARTS
    pairs = ((result, result_hbm), (d_gate, d_gate_hbm), (d_sig, d_sig_hbm))

    def writes(part):
        rows = pl.ds(part * step, step)
        return [
            pltpu.make_async_copy(src.at[rows, :], dst.at[rows, :], out_sem.at[part * 3 + which])
            for which, (src, dst) in enumerate(pairs)
        ]

    def tally(hits):
        lanes = jnp.sum(hits.astype(F32), axis=0, keepdims=True)
        return jnp.sum(lanes, axis=1, keepdims=True)

    slots = grad.shape[0]
    owner = spot_ref[spot_ref.shape[0] // 2 :, :]
    me = own_ref[4:5, :]
    slot = iota((slots, half), 0).astype(F32)
    first = tally(owner < me)
    count = tally(owner == me)
    source = slot + first
    source = jnp.where(source >= half, source - half, source)
    chosen = jnp.where((iota((slots, half), 1).astype(F32) == source) & (slot < count), 1.0, 0.0).astype(B16)
    table = jnp.concatenate([take(4), take(5)], axis=1)
    grad[...] = jnp.dot(chosen, table, preferred_element_type=F32)
    grad_copy = pltpu.make_async_copy(grad, grad_hbm, grad_sem.at[0])
    grad_copy.start()
    lane = iota((step, LANES), 1).astype(F32)
    none = jnp.zeros((step, LANES), B16)

    def turned(ref, part):
        few = step // LANES
        lines = [jnp.broadcast_to(ref[part * few + i : part * few + i + 1, :], (LANES, LANES)).T for i in range(few)]
        return jnp.concatenate(lines, axis=0)

    for part in range(PACK_PARTS):
        rows = slice(part * step, (part + 1) * step)
        spot = turned(spot_ref, part)
        skip = turned(skip_ref, part)
        gate = gate_ref[rows, :].astype(F32)
        cot = cot_ref[rows, :].astype(F32)
        block = jnp.floor(spot * (1.0 / LANES))
        mark = jnp.where(lane == spot - block * LANES, 1.0, 0.0).astype(B16)
        block = block.astype(B16)
        lines = [jnp.where(block == line, mark, none) for line in range(channels // LANES)]
        both = jnp.dot(jnp.concatenate(lines, axis=1), arrived, preferred_element_type=F32)
        mixed = both[:, 0:LANES] + skip * sig_ref[rows, :].astype(F32)
        result[rows, :] = (gate * mixed).astype(B16)
        d_gate[rows, :] = (cot * mixed).astype(B16)
        d_sig[rows, :] = (skip * (cot * gate) + both[:, LANES:]).astype(B16)
        for copy in writes(part):
            copy.start()

    for part in range(PACK_PARTS):
        for copy in writes(part):
            copy.wait()
    grad_copy.wait()


def finish(own, returned, sig, gate, cot, skip, spots, slots):
    data = jax.ShapeDtypeStruct(gate.shape, B16)
    held = pltpu.VMEM(gate.shape, B16)
    return pl.pallas_call(
        finish_body,
        in_specs=[VM] * 7,
        out_specs=(HB,) * 4,
        out_shape=(data, data, data, jax.ShapeDtypeStruct((slots, 2 * LANES), F32)),
        scratch_shapes=[
            pltpu.VMEM(returned.shape, F32),
            held,
            held,
            held,
            pltpu.VMEM((slots, 2 * LANES), F32),
            pltpu.SemaphoreType.DMA((3 * PACK_PARTS,)),
            pltpu.SemaphoreType.DMA((1,)),
        ],
        compiler_params=PARAMS,
        name="finish",
    )(own, returned, sig, gate, cot, skip.reshape(-1, LANES), spots)


def exchange(array, rows):
    parts = lax.all_to_all(
        array.reshape(-1, rows, LANES), ("ctx", "dp"), split_axis=0, concat_axis=0, tiled=True
    )
    return parts.reshape(array.shape)


def shards(signal, gate, cotangent, w_in, w_mid, w_out, rates, skip, lengths, owner):
    ctx_count = lax.axis_size("ctx")
    dp_count = lax.axis_size("dp")
    ctx_place = lax.axis_index("ctx")
    channels, local_len = signal.shape[1:]
    seq_len = local_len * ctx_count
    norm = 1.0 / math.sqrt(seq_len * dp_count)
    place = ctx_place * dp_count + lax.axis_index("dp")

    sig, gat, cot = signal[0], gate[0], cotangent[0]
    owner = owner.reshape(-1, LANES)
    packed, spots = pack(owner, sig, gat, cot, ctx_count)
    arrived = exchange(packed, 4)

    features = w_in.shape[1]
    padded = -(-features // 16) * 16
    table = np.zeros((padded, seq_len), ml_dtypes.bfloat16)
    table[:features] = embed_table(seq_len, features)
    w_in_wide = jnp.pad(w_in, ((0, 0), (0, padded - features)))
    ahead, own = make_tables(
        jnp.stack([place, ctx_place]).astype(jnp.int32), jnp.asarray(table), w_in_wide, w_mid, w_out, rates, lengths, spots
    )
    outs = convolve(own, arrived, ahead, norm)
    returned = exchange(outs, 2)
    result, d_gate, d_signal, tap_grad = finish(
        own, returned, sig, gat, cot, skip, spots, 2 * channels // ctx_count
    )
    return (result[None], d_gate[None], d_signal[None], tap_grad)


def solution(mesh):
    data = P("dp", None, "ctx")
    return jax.shard_map(
        shards,
        mesh=mesh,
        in_specs=(data, data, data, P(), P(), P(), P(), P(), P(), P()),
        out_specs=(data, data, data, P("ctx", "dp")),
        check_vma=False,
    )
```

```python
import math

import numpy as np

import jax
import jax.numpy as jnp
import ml_dtypes
from jax import lax
from jax.experimental import pallas as pl
from jax.experimental.pallas import tpu as pltpu
from jax.sharding import PartitionSpec as P

LANES = 128
PACK_PARTS = 4
VMEM_LIMIT = 16 * 1024 * 1024
F32 = jnp.float32
B16 = jnp.bfloat16
PARAMS = pltpu.CompilerParams(vmem_limit_bytes=VMEM_LIMIT)
VM = pl.BlockSpec(memory_space=pltpu.VMEM)
SM = pl.BlockSpec(memory_space=pltpu.SMEM)
HB = pl.BlockSpec(memory_space=pltpu.HBM)


def far(*arrays):
    return [pltpu.with_memory_space_constraint(array, pltpu.HBM) for array in arrays]


def iota(shape, axis):
    return lax.broadcasted_iota(jnp.int32, shape, axis)


def flip_matrix():
    return (iota((LANES, LANES), 0) + iota((LANES, LANES), 1) == LANES - 1).astype(F32).astype(B16)


def embed_table(seq_total, features):
    bands = (features - 1) // 2
    points = np.arange(seq_total, dtype=np.int64)
    freq_ids = np.arange(1, bands + 1, dtype=np.int64)
    phase = (freq_ids[:, None] * points[None, :] % seq_total).astype(np.float32) * np.float32(
        2.0 * math.pi / seq_total
    )
    ramp = points.astype(np.float32)[None, :] / np.float32(seq_total)
    table = np.concatenate([ramp, np.cos(phase), np.sin(phase)], axis=0)
    return table.astype(ml_dtypes.bfloat16)


def sine(x):
    turns = jnp.round(x * (1.0 / math.pi))
    r = x - turns * 3.140625
    r = r - turns * 9.67502593994140625e-4
    r = r - turns * 1.509957990978376432e-7
    half = turns * 0.5
    sign = 1.0 - 4.0 * (half - jnp.floor(half))
    s = r * r
    p = -1.0 / 39916800.0
    p = p * s + 1.0 / 362880.0
    p = p * s - 1.0 / 5040.0
    p = p * s + 1.0 / 120.0
    p = p * s - 1.0 / 6.0
    return sign * (r + r * s * p)


def owner_order(owner, holders):
    above = (iota((LANES, LANES), 0) < iota((LANES, LANES), 1)).astype(F32).astype(B16)
    before = (iota((holders, holders), 1) < iota((holders, holders), 0)).astype(F32).astype(B16)
    holder = iota((holders, LANES), 0)
    marks = []
    ahead = []
    seen = jnp.zeros((holders, 1), F32)
    for line in range(owner.shape[0]):
        mark = (holder == owner[line : line + 1, :]).astype(F32)
        marks.append(mark)
        ahead.append(jnp.dot(mark.astype(B16), above, preferred_element_type=F32) + seen)
        seen = seen + jnp.sum(mark, axis=1, keepdims=True)
    total = jnp.broadcast_to(seen, (holders, LANES)).astype(B16)
    start = jnp.dot(before, total, preferred_element_type=F32)
    return [jnp.sum(m * (a + start), axis=0, keepdims=True) for m, a in zip(marks, ahead)]


def pack_body(
    owner_hbm, sig_hbm, gate_hbm, cot_hbm, out_hbm, spot_ref,
    owner_in, sig_in, gate_in, cot_in, wide, out, owner_sem, in_sem, out_sem, *, holders
):
    channels = sig_in.shape[0]
    half = channels // 2
    step = channels // PACK_PARTS
    pairs = ((sig_hbm, sig_in), (gate_hbm, gate_in), (cot_hbm, cot_in))

    reads = [pltpu.make_async_copy(src, dst, in_sem.at[which]) for which, (src, dst) in enumerate(pairs)]

    def write(part):
        rows = pl.ds(part * 2 * step, 2 * step)
        return pltpu.make_async_copy(out.at[rows, :], out_hbm.at[rows, :], out_sem.at[part])

    owner_copy = pltpu.make_async_copy(owner_hbm, owner_in, owner_sem.at[0])
    owner_copy.start()
    for copy in reads:
        copy.start()
    owner_copy.wait()
    spots = owner_order(owner_in[...], holders)
    for line, spot in enumerate(spots):
        spot_ref[line : line + 1, :] = spot
    spot_ref[len(spots) :, :] = owner_in[...].astype(F32)
    for copy in reads:
        copy.wait()
    back = (cot_in[...].astype(F32) * gate_in[...].astype(F32)).astype(B16)
    values = jnp.concatenate([sig_in[...], back], axis=1)
    few = step // 2
    row = iota((LANES, LANES), 0).astype(F32).astype(B16)
    one = jnp.ones((LANES, LANES), B16)
    none = jnp.zeros((LANES, LANES), B16)

    def onehot(block, spot):
        low = spot - block * LANES
        low = jnp.where((low >= 0) & (low < LANES), low, 2.0 * LANES).astype(B16)
        return jnp.where(row == low, one, none)

    for part in range(PACK_PARTS):
        chosen = []
        for side in range(2):
            for block in range(few // LANES):
                block += (side * half + part * few) // LANES
                chosen.append(jnp.concatenate([onehot(block, spot) for spot in spots], axis=1))
        moved = jnp.dot(jnp.concatenate(chosen, axis=0), values, preferred_element_type=F32)
        for side in range(2):
            rows = slice(side * few, (side + 1) * few)
            wide[pl.ds(4 * few * part + side, few, stride=4), :] = moved[rows, 0:LANES]
            wide[pl.ds(4 * few * part + 2 + side, few, stride=4), :] = moved[rows, LANES:]
        rows = slice(part * 2 * step, (part + 1) * 2 * step)
        out[rows, :] = wide[rows, :].astype(B16)
        write(part).start()
    for part in range(PACK_PARTS):
        write(part).wait()


def pack(owner, sig, gate, cot, holders):
    rows = 2 * sig.shape[0]
    held = pltpu.VMEM(sig.shape, B16)
    lines = owner.shape[0]
    return pl.pallas_call(
        lambda *refs: pack_body(*refs, holders=holders),
        in_specs=[HB] * 4,
        out_specs=(HB, VM),
        out_shape=(jax.ShapeDtypeStruct((rows, LANES), B16), jax.ShapeDtypeStruct((2 * lines, LANES), F32)),
        scratch_shapes=[
            pltpu.VMEM(owner.shape, jnp.int32),
            held,
            held,
            held,
            pltpu.VMEM((rows, LANES), F32),
            pltpu.VMEM((rows, LANES), B16),
            pltpu.SemaphoreType.DMA((1,)),
            pltpu.SemaphoreType.DMA((3,)),
            pltpu.SemaphoreType.DMA((PACK_PARTS,)),
        ],
        compiler_params=PARAMS,
        name="pack",
    )(*far(owner, sig, gate, cot))


def tables_body(
    place_ref, emb_hbm, w_in_ref, w_mid_hbm, w_out_hbm, rate_hbm, len_hbm, spot_ref, ahead_ref, own_ref,
    emb_ref, w_mid_ref, w_out_ref, rate_ref, len_ref, taps, in_sem
):
    seq_len = emb_ref.shape[1]
    width = 512
    blocks = seq_len // LANES
    channels = w_out_ref.shape[1]
    lines = channels // LANES
    pairs = (
        (rate_hbm, rate_ref), (len_hbm, len_ref), (w_out_hbm, w_out_ref), (w_mid_hbm, w_mid_ref), (emb_hbm, emb_ref)
    )
    copies = [pltpu.make_async_copy(src, dst, in_sem.at[which]) for which, (src, dst) in enumerate(pairs)]
    for copy in copies:
        copy.start()
    for copy in copies:
        copy.wait()
    target = (iota((8, LANES), 0) * (channels // 2) + place_ref[0]).astype(F32)
    marks = [jnp.where(spot_ref[line : line + 1, :] == target, 1.0, 0.0) for line in range(lines)]

    def chosen(ref, first=0):
        total = 0.0
        for line in range(lines):
            total = total + marks[line] * ref[first + line : first + line + 1, :].astype(F32)
        return jnp.sum(total, axis=1, keepdims=True)

    rate = chosen(rate_ref)
    length = chosen(len_ref)
    own_ref[0:2, :] = jnp.broadcast_to(length[0:2, :], (2, LANES))
    own_ref[2:4, :] = jnp.broadcast_to(chosen(spot_ref, lines)[0:2, :], (2, LANES))
    own_ref[4:8, :] = jnp.full((4, LANES), place_ref[1], jnp.int32).astype(F32)
    scale = lax.rsqrt(jnp.maximum(length, 1.0))
    w_in = w_in_ref[...]
    w_mid = w_mid_ref[...]
    w_out = lax.dot_general(
        jnp.concatenate(marks, axis=1).astype(B16), w_out_ref[...], (((1,), (1,)), ((), ())), preferred_element_type=F32
    ).astype(B16)
    taps[0:8, :] = jnp.zeros((8, LANES), F32)
    for part in range(seq_len // width):
        emb = emb_ref[:, part * width : (part + 1) * width]
        one = sine(jnp.dot(w_in, emb, preferred_element_type=F32)).astype(B16)
        two = sine(jnp.dot(w_mid, one, preferred_element_type=F32)).astype(B16)
        net = jnp.dot(w_out, two, preferred_element_type=F32)
        point = (part * width + iota((8, width), 1)).astype(F32)
        decay = jnp.exp(-rate * point / seq_len)
        value = jnp.where(point < length, net * decay * scale, 0.0).astype(B16)
        for piece in range(width // LANES):
            block = part * (width // LANES) + piece + 1
            here = value[:, piece * LANES : (piece + 1) * LANES]
            taps[block * 8 : block * 8 + 8, :] = here.astype(F32)
    lane = iota((8, LANES), 1)
    sub = iota((8, LANES), 0)
    build_key = jnp.where(lane >= sub, lane, lane + LANES)

    def head(row):
        spread = jnp.broadcast_to(taps[row : row + 1, :], (8, LANES))
        return pltpu.roll(spread, 0, 1, stride=1, stride_axis=0)

    def fill(spot, low, high):
        built = []
        for a in range(LANES // 8):
            piece = jnp.where(build_key >= LANES - 8 * a, low, high)
            built.append(pltpu.roll(piece, 8 * a, 1) if a else piece)
        ahead_ref[spot * LANES : (spot + 1) * LANES, :] = jnp.concatenate(built, axis=0).astype(B16)

    for c in range(2):
        low = head(0)
        for k in range(blocks):
            high = head((k + 1) * 8 + c)
            fill(c * blocks + k, low, high)
            low = high


def make_tables(place, emb, w_in, w_mid, w_out, rate, length, spots):
    blocks = emb.shape[1] // LANES
    rate = rate.reshape(-1, LANES)
    length = length.reshape(-1, LANES)
    w_out = w_out.T
    held = [pltpu.VMEM(array.shape, array.dtype) for array in (emb, w_mid, w_out, rate, length)]
    emb, w_mid, w_out, rate, length = far(emb, w_mid, w_out, rate, length)
    return pl.pallas_call(
        tables_body,
        in_specs=[SM, HB, VM, HB, HB, HB, HB, VM],
        out_specs=(VM, VM),
        out_shape=(
            jax.ShapeDtypeStruct((2 * blocks * LANES, LANES), B16),
            jax.ShapeDtypeStruct((8, LANES), F32),
        ),
        scratch_shapes=[*held, pltpu.VMEM(((blocks + 1) * 8, LANES), F32), pltpu.SemaphoreType.DMA((5,))],
        compiler_params=PARAMS,
        name="tables",
    )(place, emb, w_in, w_mid, w_out, rate, length, spots)


def diagonal(here, after, key):
    total = None
    for a in range(LANES // 8):
        rows = slice(8 * a, 8 * a + 8)
        late = 0.0 if after is None else after[rows, :]
        piece = jnp.where(key >= LANES - 8 * a, late, here[rows, :])
        if a:
            piece = pltpu.roll(piece, 8 * a, 1)
        total = piece if total is None else total + piece
    total = pltpu.roll(total, 0, 1, stride=1, stride_axis=0)
    return jnp.sum(total, axis=0, keepdims=True)


def convolve_body(own_ref, arr_ref, ahead_ref, out, wide, sig, back, lags, spread, *, norm):
    peers = arr_ref.shape[0] // 4
    blocks = ahead_ref.shape[0] // (2 * LANES)
    batch = peers // blocks
    pairs = blocks // 2
    count = pairs * batch
    pad = sig.shape[2] - count
    part = pairs // 2
    flip = flip_matrix()
    key = iota((8, LANES), 0) + iota((8, LANES), 1)
    wide[...] = arr_ref[...].astype(F32)
    zero = jnp.zeros((pad, LANES), B16)
    empty = jnp.zeros((LANES, LANES), B16)

    for c in range(2):
        x = wide[pl.ds(c, peers, stride=4), :].astype(B16).reshape(pairs, 2, batch, LANES)
        b = jnp.dot(wide[pl.ds(2 + c, peers, stride=4), :].astype(B16), flip, preferred_element_type=F32)
        b = b.astype(B16).reshape(pairs, 2, batch, LANES)
        for e in range(2):
            sig[c, e, 0:pad, :] = zero
            sig[c, e, pad:, :] = x[:, e].reshape(count, LANES)
            back[c, e, 0:count, :] = b[:, e].reshape(count, LANES)
            back[c, e, count:, :] = zero

    def send(c, row, first, value):
        for i in range(value.shape[0] // batch):
            for e in range(2):
                peer = (2 * (first + i) + e) * batch
                spread[pl.ds(6 * peer + row + c, batch, stride=6), :] = value[
                    i * batch : (i + 1) * batch, e * LANES : (e + 1) * LANES
                ]

    for c in range(2):

        def table(k):
            spot = (c * blocks + k) * LANES
            return ahead_ref[spot : spot + LANES, :] if k >= 0 else empty

        def grid(*tables):
            rows = [jnp.concatenate([table(k) for k in line], axis=1) for line in tables]
            return jnp.concatenate(rows, axis=0)

        def earlier(first, m):
            rows = slice(pad + (first - m) * batch, pad + (first - m + part) * batch)
            return [sig[c, 0, rows, :], sig[c, 1, rows, :]]

        def later(first, m):
            rows = slice((first + m) * batch, (first + m + part) * batch)
            return [back[c, 0, rows, :], back[c, 1, rows, :]]

        turned = [sig[c, e, pad:, :].astype(F32).T.astype(B16) for e in range(2)]
        before = None
        for first in range(0, pairs, 4):
            rows = count if first < part else count // 2
            upper = []
            lower = []
            for m in range(first, first + 4):
                here = slice(m * batch, m * batch + rows)
                next_ = slice((m + 1) * batch, (m + 1) * batch + rows)
                upper += [back[c, 0, here, :], back[c, 1, here, :]]
                lower += [back[c, 1, here, :], back[c, 0, next_, :]]
            right = jnp.concatenate([jnp.concatenate(upper, axis=1), jnp.concatenate(lower, axis=1)], axis=0)
            left = jnp.concatenate([side[:, 0:rows] for side in turned], axis=1)
            outer = jnp.dot(left, right, preferred_element_type=F32)
            for j in range(8):
                now = outer[:, j * LANES : (j + 1) * LANES]
                if before is not None:
                    spot = c * blocks + 2 * first + j - 1
                    lags[spot : spot + 1, :] = diagonal(before, now, key)
                before = now
        lags[(c + 1) * blocks - 1 : (c + 1) * blocks, :] = diagonal(before, None, key)
        for first in range(0, pairs, part):
            deep = range(first + part)
            left = jnp.concatenate([piece for m in deep for piece in earlier(first, m)], axis=1)
            right = [grid((2 * m, 2 * m + 1), (2 * m - 1, 2 * m)) for m in deep]
            send(c, 0, first, jnp.dot(left, jnp.concatenate(right, axis=0), preferred_element_type=F32))
            deep = range(pairs - first)
            left = jnp.concatenate([piece for m in deep for piece in later(first, m)], axis=1)
            right = [grid((2 * m, 2 * m - 1), (2 * m + 1, 2 * m)) for m in deep]
            send(c, 2, first, jnp.dot(left, jnp.concatenate(right, axis=0), preferred_element_type=F32))
    point = (iota((blocks, LANES), 0) * LANES + iota((blocks, LANES), 1)).astype(F32)
    holder = jnp.concatenate([jnp.full((batch, LANES), h, jnp.int32) for h in range(blocks)], axis=0).astype(F32)
    ordered = jnp.dot((lags[...] * norm).astype(B16), flip, preferred_element_type=F32)
    for c in range(2):
        here = slice(c * blocks, (c + 1) * blocks)
        lags[here, :] = jnp.where(point < own_ref[c : c + 1, :], ordered[here, :], 0.0)
    for half in range(2):
        total = jnp.zeros((peers, LANES), F32)
        for c in range(2):
            column = lags[pl.ds(c * blocks + half, batch, stride=2), :]
            column = jnp.concatenate([column] * blocks, axis=0)
            total = jnp.where(holder == own_ref[2 + c : 3 + c, :], column, total)
        spread[pl.ds(4 + half, peers, stride=6), :] = total
    out[...] = spread[...].astype(B16)


def convolve(own, arrived, ahead, norm):
    peers = arrived.shape[0] // 4
    blocks = ahead.shape[0] // (2 * LANES)
    rows = peers // 2 + LANES
    body = lambda *refs: convolve_body(*refs, norm=norm)
    return pl.pallas_call(
        body,
        in_specs=[VM, VM, VM],
        out_specs=VM,
        out_shape=jax.ShapeDtypeStruct((6 * peers, LANES), B16),
        scratch_shapes=[
            pltpu.VMEM((4 * peers, LANES), F32),
            pltpu.VMEM((2, 2, rows, LANES), B16),
            pltpu.VMEM((2, 2, rows, LANES), B16),
            pltpu.VMEM((2 * blocks, LANES), F32),
            pltpu.VMEM((6 * peers, LANES), F32),
        ],
        compiler_params=PARAMS,
        name="convolve",
    )(own, arrived, ahead)


def finish_body(
    own_ref, ret_ref, sig_ref, gate_ref, cot_ref, skip_ref, spot_ref,
    result_hbm, d_gate_hbm, d_sig_hbm, grad_hbm, wide, result, d_gate, d_sig, grad, out_sem, grad_sem
):
    wide[...] = ret_ref[...].astype(F32)
    channels = gate_ref.shape[0]
    half = channels // 2

    def take(row):
        return wide[pl.ds(row, half, stride=6), :].astype(B16)

    flip = flip_matrix()

    def ordered(row):
        return jnp.dot(take(row), flip, preferred_element_type=F32).astype(B16)

    sides = [jnp.concatenate([take(c), ordered(2 + c)], axis=1) for c in range(2)]
    arrived = jnp.concatenate(sides, axis=0)
    step = channels // PACK_PARTS
    pairs = ((result, result_hbm), (d_gate, d_gate_hbm), (d_sig, d_sig_hbm))

    def writes(part):
        rows = pl.ds(part * step, step)
        return [
            pltpu.make_async_copy(src.at[rows, :], dst.at[rows, :], out_sem.at[part * 3 + which])
            for which, (src, dst) in enumerate(pairs)
        ]

    def tally(hits):
        lanes = jnp.sum(hits.astype(F32), axis=0, keepdims=True)
        return jnp.sum(lanes, axis=1, keepdims=True)

    slots = grad.shape[0]
    owner = spot_ref[spot_ref.shape[0] // 2 :, :]
    me = own_ref[4:5, :]
    slot = iota((slots, half), 0).astype(F32)
    first = tally(owner < me)
    count = tally(owner == me)
    source = slot + first
    source = jnp.where(source >= half, source - half, source)
    chosen = jnp.where((iota((slots, half), 1).astype(F32) == source) & (slot < count), 1.0, 0.0).astype(B16)
    table = jnp.concatenate([take(4), take(5)], axis=1)
    grad[...] = jnp.dot(chosen, table, preferred_element_type=F32)
    grad_copy = pltpu.make_async_copy(grad, grad_hbm, grad_sem.at[0])
    grad_copy.start()
    lane = iota((step, LANES), 1).astype(F32)
    none = jnp.zeros((step, LANES), B16)

    def turned(ref, part):
        few = step // LANES
        lines = [jnp.broadcast_to(ref[part * few + i : part * few + i + 1, :], (LANES, LANES)).T for i in range(few)]
        return jnp.concatenate(lines, axis=0)

    for part in range(PACK_PARTS):
        rows = slice(part * step, (part + 1) * step)
        spot = turned(spot_ref, part)
        skip = turned(skip_ref, part)
        gate = gate_ref[rows, :].astype(F32)
        cot = cot_ref[rows, :].astype(F32)
        block = jnp.floor(spot * (1.0 / LANES))
        mark = jnp.where(lane == spot - block * LANES, 1.0, 0.0).astype(B16)
        block = block.astype(B16)
        lines = [jnp.where(block == line, mark, none) for line in range(channels // LANES)]
        both = jnp.dot(jnp.concatenate(lines, axis=1), arrived, preferred_element_type=F32)
        mixed = both[:, 0:LANES] + skip * sig_ref[rows, :].astype(F32)
        result[rows, :] = (gate * mixed).astype(B16)
        d_gate[rows, :] = (cot * mixed).astype(B16)
        d_sig[rows, :] = (skip * (cot * gate) + both[:, LANES:]).astype(B16)
        for copy in writes(part):
            copy.start()

    for part in range(PACK_PARTS):
        for copy in writes(part):
            copy.wait()
    grad_copy.wait()


def finish(own, returned, sig, gate, cot, skip, spots, slots):
    data = jax.ShapeDtypeStruct(gate.shape, B16)
    held = pltpu.VMEM(gate.shape, B16)
    return pl.pallas_call(
        finish_body,
        in_specs=[VM] * 7,
        out_specs=(HB,) * 4,
        out_shape=(data, data, data, jax.ShapeDtypeStruct((slots, 2 * LANES), F32)),
        scratch_shapes=[
            pltpu.VMEM(returned.shape, F32),
            held,
            held,
            held,
            pltpu.VMEM((slots, 2 * LANES), F32),
            pltpu.SemaphoreType.DMA((3 * PACK_PARTS,)),
            pltpu.SemaphoreType.DMA((1,)),
        ],
        compiler_params=PARAMS,
        name="finish",
    )(own, returned, sig, gate, cot, skip.reshape(-1, LANES), spots)


def exchange(array, rows):
    parts = lax.all_to_all(
        array.reshape(-1, rows, LANES), ("ctx", "dp"), split_axis=0, concat_axis=0, tiled=True
    )
    return parts.reshape(array.shape)


def shards(signal, gate, cotangent, w_in, w_mid, w_out, rates, skip, lengths, owner):
    ctx_count = lax.axis_size("ctx")
    dp_count = lax.axis_size("dp")
    ctx_place = lax.axis_index("ctx")
    channels, local_len = signal.shape[1:]
    seq_len = local_len * ctx_count
    norm = 1.0 / math.sqrt(seq_len * dp_count)
    place = ctx_place * dp_count + lax.axis_index("dp")

    sig, gat, cot = signal[0], gate[0], cotangent[0]
    owner = owner.reshape(-1, LANES)
    packed, spots = pack(owner, sig, gat, cot, ctx_count)
    arrived = exchange(packed, 4)

    features = w_in.shape[1]
    padded = -(-features // 16) * 16
    table = np.zeros((padded, seq_len), ml_dtypes.bfloat16)
    table[:features] = embed_table(seq_len, features)
    w_in_wide = jnp.pad(w_in, ((0, 0), (0, padded - features)))
    ahead, own = make_tables(
        jnp.stack([place, ctx_place]).astype(jnp.int32), jnp.asarray(table), w_in_wide, w_mid, w_out, rates, lengths, spots
    )
    outs = convolve(own, arrived, ahead, norm)
    returned = exchange(outs, 2)
    result, d_gate, d_signal, tap_grad = finish(
        own, returned, sig, gat, cot, skip, spots, 2 * channels // ctx_count
    )
    return (result[None], d_gate[None], d_signal[None], tap_grad)


def solution(mesh):
    data = P("dp", None, "ctx")
    return jax.shard_map(
        shards,
        mesh=mesh,
        in_specs=(data, data, data, P(), P(), P(), P(), P(), P(), P()),
        out_specs=(data, data, data, P("ctx", "dp")),
        check_vma=False,
    )
```
